512 devices in a mesh: ka: 16 (over y, z_hi), row: 4 (over x), col: 8 (over z_lo, core).
Axes of the slice: x: 4, y: 4, z: 16 (z_hi: 4, z_lo: 4; z = z_hi * 4 + z_lo), core: 2. Of those that a mesh axis runs over, the one named last changes fastest.
Arguments:
- exciton: bfloat16 [16, 4, 128, 128], P('ka'), may hold values from -6 to 6
- orb_cond: bfloat16 [16, 128, 2048], P('ka', None, 'row'), may hold values from -0.5 to 0.5
- orb_val: bfloat16 [16, 128, 2048], P('ka', None, 'col'), may hold values from -0.5 to 0.5
- screened: bfloat16 [16, 2048, 2048], P(None, 'row', 'col'), may hold values from -1.5 to 1.5
- q_table: int32 [16, 16], replicated, may hold values from 0 to 15, as said below
Outputs:
- applied: float32 [16, 4, 128, 128], P('ka', None, 'col')
The draws below stay inside these ranges and needn't reach their ends.
Inputs may be any that keep to these rules, and one draw needn't show every extreme that they name: q_table is the difference table of the k-points of a cyclic grid of 16 points under a relabeling of points and of differences: every row and every column holds each of 0 to 15 once.
All inputs are finite; a program needn't handle non-finite values.
Results may differ from the reference program's by a relative error of at most 0.019.
Values may be sent and summed in bfloat16 or wider, within the bound.
A program may use at most 64 MiB of HBM per device.

```python
import math
import jax
import jax.numpy as jnp
from jax import lax

NV = 128
NC = 128
NMU = 2048
NB = 4
NK = 16


def draw_q_table(key, part):
    first_key, second_key = jax.random.split(jax.random.fold_in(key, 7))
    positions = jax.random.permutation(first_key, NK).astype(jnp.int32)
    labels = jax.random.permutation(second_key, NK).astype(jnp.int32)
    difference = (positions[:, None] - positions[None, :]) % NK
    return labels[difference].astype(jnp.int32)


def shard_levels(rng, extent, shards, least, top_value):
    def one(dim, blocks):
        draws = jax.random.uniform(jax.random.fold_in(jax.random.fold_in(rng, 6), dim), (blocks,), jnp.float32, least / len(shards), top_value / len(shards))
        return jnp.repeat(jnp.exp(draws), extent[dim] // blocks).reshape((-1,) + (1,) * (len(extent) - dim - 1))

    factor_of = one(*shards[0])
    for cut in shards[1:]:
        factor_of = factor_of * one(*cut)
    return factor_of


def noise(rng, extent, deviation, reach, cuts=(), held_as=jnp.bfloat16):
    result = deviation * jax.random.normal(rng, extent, jnp.float32)
    if cuts:
        result = result * shard_levels(rng, extent, cuts, -0.22, 0.18)
    return jnp.clip(result, -reach, reach).astype(held_as)


def setup_inputs(seed: int = 0) -> dict:
    keys = jax.random.split(jax.random.key(seed), 6)
    return {
        "exciton": noise(keys[0], (NK, NB, NV, NC), 1.0, 6.0, ((0, 16),)),
        "orb_cond": noise(keys[1], (NK, NC, NMU), NC ** -0.5, 0.5, ((0, 16), (2, 4))),
        "orb_val": noise(keys[2], (NK, NV, NMU), NV ** -0.5, 0.5, ((0, 16), (2, 8))),
        "screened": noise(keys[3], (NK, NMU, NMU), NK ** -0.5, 1.5, ((1, 4), (2, 8))),
        "q_table": draw_q_table(jax.random.fold_in(keys[5], 71), 0),
    }


def reference(exciton, orb_cond, orb_val, screened, q_table):
    highest = lax.Precision.HIGHEST
    panels = jnp.einsum('kbvc,kcm->kbvm', exciton.astype(jnp.float32), orb_cond.astype(jnp.float32), precision=highest).astype(jnp.bfloat16)

    def make_pairs(k_point):
        return jnp.einsum('bvm,vn->bmn', panels[k_point].astype(jnp.float32), orb_val[k_point].astype(jnp.float32), precision=highest).astype(jnp.bfloat16)
    pair_block = lax.map(make_pairs, jnp.arange(NK, dtype=jnp.int32))
    factor = math.sqrt(NV * NC) / NMU

    def per_point(k_point):
        columns = q_table[:, k_point]

        def accumulate(running, k_other):
            weights = screened[columns[k_other]].astype(jnp.float32)
            return (running + weights[None] * pair_block[k_other].astype(jnp.float32), None)
        direct, unused = lax.scan(accumulate, jnp.zeros((NB, NMU, NMU), jnp.float32), jnp.arange(NK, dtype=jnp.int32))
        direct = direct.astype(jnp.bfloat16)
        half_sums = jnp.einsum('bmn,vn->bmv', direct.astype(jnp.float32), orb_val[k_point].astype(jnp.float32), precision=highest).astype(jnp.bfloat16)
        return jnp.einsum('cm,bmv->bvc', orb_cond[k_point].astype(jnp.float32), half_sums.astype(jnp.float32), precision=highest) * factor
    return lax.map(per_point, jnp.arange(NK, dtype=jnp.int32))
```

```python
import functools
import math

import jax
import jax.numpy as jnp
from jax import lax
from jax.experimental import pallas as pl
from jax.experimental.pallas import tpu as pltpu
from jax.sharding import PartitionSpec as P

NZH = 4
MESH = pl.DeviceIdType.MESH
BF16 = jnp.bfloat16
F32 = jnp.float32
NT = (((1,), (1,)), ((), ()))


def kernel(
    sizes, factor, q_ref, ex_hbm, cond_hbm, val_hbm, w_hbm, out_ref,
    ex_v, cond_v, condt, w_v, wf, psend, pb, vb, pairs, direct, hs, c1, tsum, zr, us, fr, xs,
    ld, p1s, p1r, p2s, p2r, pcs, pcr, v1s, v1r, vas, var, vbs, vbr, vcs, vcr, vds, vdr,
    h1s, h1r, h2s, h2r, h3s, h3r, h5s, h5r,
):
    ny, nzh, nx, nzl = sizes
    nka = ny * nzh
    a, r, c = lax.axis_index("ka"), lax.axis_index("row"), lax.axis_index("col")
    y, zh = a // nzh, a % nzh
    zl, co = c // 2, c % 2
    partner = {"col": zl * 2 + 1 - co}

    def ka(d):
        return (a + d) % nka

    def zl_of(d):
        return (zl + d) % nzl

    def y_of(d):
        return (y + d) % ny

    def zh_of(d):
        return (zh + d) % nzh

    def x_of(d):
        return (r + d) % nx

    def send(src, dst, ss, rs, where):
        pltpu.make_async_remote_copy(
            src_ref=src, dst_ref=dst, send_sem=ss, recv_sem=rs, device_id=where, device_id_type=MESH
        ).start()

    def got(ref, rs):
        pltpu.make_async_copy(ref, ref, rs).wait()

    def each(n, body):
        def step(d, carry):
            body(d)
            return carry

        lax.fori_loop(1, n, step, 0)

    load_ex = pltpu.make_async_copy(ex_hbm.at[zl], ex_v, ld.at[0])
    load_cond = pltpu.make_async_copy(cond_hbm, cond_v, ld.at[1])
    load_val = pltpu.make_async_copy(val_hbm.at[r], vb.at[a, r], ld.at[2])
    load_w = pltpu.make_async_copy(w_hbm.at[:, a], w_v, ld.at[3])
    load_val.start()
    load_cond.start()
    load_ex.start()
    load_w.start()

    barrier = pltpu.get_barrier_semaphore()

    def hello(where):
        pl.semaphore_signal(barrier, inc=1, device_id=where, device_id_type=MESH)

    each(nka, lambda d: hello({"ka": ka(d)}))
    each(nzl, lambda d: hello({"col": zl_of(d) * 2 + co}))
    each(nx, lambda d: hello({"row": x_of(d)}))
    hello(partner)

    load_cond.wait()
    load_ex.wait()
    condt[...] = cond_v[...].T
    psend[...] = (
        lax.dot_general(condt[...], ex_v[...], NT, preferred_element_type=F32)
        .astype(BF16)
        .reshape(psend.shape)
    )
    pb[a, zl, co] = psend[a, co]
    load_val.wait()
    pl.semaphore_wait(barrier, nka + nzl + nx - 2)

    def v1(d):
        send(vb.at[a, r], vb.at[a, r], v1s.at[d], v1r.at[d], {"ka": y * nzh + zh_of(d)})

    each(nzh, v1)

    def p1(d):
        send(psend.at[ka(d), co], pb.at[a, zl, co], p1s.at[d], p1r.at[d], {"ka": ka(d)})

    each(nka, p1)

    load_w.wait()
    wf[...] = w_v[...].astype(F32)

    each(nzh, lambda d: got(vb.at[a, r], v1r.at[d]))
    mine = pl.ds(y * nzh, nzh)

    def v2a(d):
        part = vb.at[mine, r, 0]
        send(part, part, vas.at[d], var.at[d], {"ka": y_of(d) * nzh + zh})

    def v2b(d):
        part = vb.at[mine, r, 1]
        send(part, part, vbs.at[d], vbr.at[d], {"row": x_of(d)})

    each(ny, v2a)
    each(nx, v2b)

    each(nka, lambda d: got(pb.at[a, zl, co], p1r.at[d]))

    def p2(d):
        part = pb.at[:, zl, co]
        send(part, part, p2s.at[d], p2r.at[d], {"col": zl_of(d) * 2 + co})

    def pc(d):
        part = pb.at[:, (zl + nzl - d) % nzl, co]
        send(part, part, pcs.at[d], pcr.at[d], partner)

    each(nzl, p2)
    pc(0)

    each(ny, lambda d: got(vb.at[mine, r, 0], var.at[d]))

    def v3a(d):
        part = vb.at[:, r, 0]
        send(part, part, vcs.at[d], vcr.at[d], {"row": x_of(d)})

    each(nx, v3a)
    each(nx, lambda d: got(vb.at[mine, r, 1], vbr.at[d]))

    def v3b(d):
        part = vb.at[mine, :, 1]
        send(part, part, vds.at[d], vdr.at[d], {"ka": y_of(d) * nzh + zh})

    each(ny, v3b)

    def p2_got(d):
        got(pb.at[:, zl, co], p2r.at[d])
        pc(d)

    each(nzl, p2_got)
    got(pb.at[:, zl, co], pcr.at[0])
    each(nzl, lambda d: got(pb.at[:, zl, co], pcr.at[d]))
    each(nx, lambda d: got(vb.at[:, r, 0], vcr.at[d]))
    each(ny, lambda d: got(vb.at[mine, :, 1], vdr.at[d]))

    rows, nv, nnu = nzl * 32, nzl * 32, vb.shape[-1]

    def pair(k, carry):
        panel = pb[k].reshape(rows, nv)
        val = vb[k].reshape(nv, nnu)
        pairs[k] = jnp.dot(panel, val, preferred_element_type=F32).reshape(nzl, 32, nnu)
        return carry

    lax.fori_loop(0, nka, pair, 0)

    kg = min(8, nka)
    lanes = nnu // 128

    def weigh(t, carry):
        g = t // (4 * lanes)
        s = pl.ds(pl.multiple_of(((t // lanes) % 4) * 8, 8), 8)
        l = pl.ds(pl.multiple_of((t % lanes) * 128, 128), 128)
        sums = [[None] * nzl for _ in range(kg)]
        for k2 in range(nka):
            p = [pairs[k2, b, s, l] for b in range(nzl)]
            for i in range(kg):
                w = wf[q_ref[k2, g * kg + i], s, l]
                for b in range(nzl):
                    term = w * p[b]
                    sums[i][b] = term if k2 == 0 else sums[i][b] + term
        for i in range(kg):
            for b in range(nzl):
                direct[g * kg + i, b, s, l] = sums[i][b]
        return carry

    lax.fori_loop(0, (nka // kg) * 4 * lanes, weigh, 0)

    def half(k, carry):
        d = direct[k].reshape(rows, nnu).astype(BF16)
        val = vb[k].reshape(nv, nnu)
        h = lax.dot_general(val, d, NT, preferred_element_type=F32)
        hs[k] = h.astype(BF16).reshape(nzl, 2, 16, rows)
        return carry

    lax.fori_loop(0, nka, half, 0)

    send(hs.at[:, :, 1 - co], c1, h1s.at[0], h1r.at[0], partner)
    got(c1, h1r.at[0])

    def add_core(k, carry):
        tsum[:, k] = (hs[k, :, co].astype(F32) + c1[k].astype(F32)).astype(BF16)
        return carry

    lax.fori_loop(0, nka, add_core, 0)

    def h2(d):
        send(tsum.at[zl_of(d)], zr.at[d], h2s.at[d], h2r.at[d], {"col": zl_of(d) * 2 + co})

    each(nzl, h2)
    each(nzl, lambda d: got(zr.at[d], h2r.at[d]))

    def add_zl(k, carry):
        total = tsum[zl, k].astype(F32)
        for d in range(1, nzl):
            total = total + zr[d, k].astype(F32)
        us[k] = total.astype(BF16)
        return carry

    lax.fori_loop(0, nka, add_zl, 0)

    def h3(d):
        send(us.at[ka(d)], fr.at[a], h3s.at[d], h3r.at[d], {"ka": ka(d)})

    each(nka, h3)
    fr[a] = us[a]
    each(nka, lambda d: got(fr.at[a], h3r.at[d]))

    lane_b = lax.broadcasted_iota(jnp.int32, (16, rows), 1) // 32

    def last(k, total):
        f = fr[k].astype(F32)
        lhs = jnp.concatenate(
            [jnp.where(lane_b == b, f, 0.0) for b in range(nzl)], axis=0
        ).astype(BF16)
        ct = condt[pl.ds(pl.multiple_of(k * 32, 32), 32), :]
        rhs = jnp.concatenate([ct] * nzl, axis=0)
        return total + jnp.dot(lhs, rhs, preferred_element_type=F32)

    total = lax.fori_loop(0, nka, last, jnp.zeros((nzl * 16, condt.shape[1]), F32))
    xs[r] = total.astype(BF16)

    def h5(d):
        send(xs.at[r], xs.at[r], h5s.at[d], h5r.at[d], {"row": x_of(d)})

    each(nx, h5)
    each(nx, lambda d: got(xs.at[r], h5r.at[d]))
    result = xs[0].astype(F32)
    for i in range(1, nx):
        result = result + xs[i].astype(F32)
    out_ref[...] = (result * factor).reshape(out_ref.shape)

    each(nzh, lambda d: got(vb.at[a, r], v1s.at[d]))
    each(nka, lambda d: got(pb.at[a, zl, co], p1s.at[d]))
    each(ny, lambda d: got(vb.at[mine, r, 0], vas.at[d]))
    each(nx, lambda d: got(vb.at[mine, r, 1], vbs.at[d]))
    each(nzl, lambda d: got(pb.at[:, zl, co], p2s.at[d]))
    got(pb.at[:, zl, co], pcs.at[0])
    each(nzl, lambda d: got(pb.at[:, zl, co], pcs.at[d]))
    each(nx, lambda d: got(vb.at[:, r, 0], vcs.at[d]))
    each(ny, lambda d: got(vb.at[mine, :, 1], vds.at[d]))
    got(c1, h1s.at[0])
    each(nzl, lambda d: got(zr.at[d], h2s.at[d]))
    each(nka, lambda d: got(fr.at[a], h3s.at[d]))
    each(nx, lambda d: got(xs.at[r], h5s.at[d]))


def local(sizes, factor, exciton, orb_cond, orb_val, screened, q_table):
    ny, nzh, nx, nzl = sizes
    nka = ny * nzh
    nc = exciton.shape[-1]
    nv = nzl * 32
    rows = nzl * 32
    mu = nka * 32
    nnu = orb_val.shape[-1]
    any_space = pl.BlockSpec(memory_space=pl.ANY)
    dma = lambda n: pltpu.SemaphoreType.DMA((n,))
    vm = pltpu.VMEM
    out = pl.pallas_call(
        functools.partial(kernel, sizes, factor),
        name="isdf_direct",
        out_shape=jax.ShapeDtypeStruct((nzl, 16, nc), F32),
        in_specs=[pl.BlockSpec(memory_space=pltpu.SMEM)] + [any_space] * 4,
        out_specs=pl.BlockSpec(memory_space=pltpu.VMEM),
        scratch_shapes=[
            vm((nv, nc), BF16),
            vm((nc, mu), BF16),
            vm((mu, nc), BF16),
            vm((nka, 32, nnu), BF16),
            vm((nka, 32, nnu), F32),
            vm((nka, 2, 16, nv), BF16),
            vm((nka, nzl, 2, 16, nv), BF16),
            vm((nka, nx, 2, 16, nnu), BF16),
            vm((nka, nzl, 32, nnu), F32),
            vm((nka, nzl, 32, nnu), F32),
            vm((nka, nzl, 2, 16, rows), BF16),
            vm((nka, nzl, 16, rows), BF16),
            vm((nzl, nka, 16, rows), BF16),
            vm((nzl, nka, 16, rows), BF16),
            vm((nka, 16, rows), BF16),
            vm((nka, 16, rows), BF16),
            vm((nx, nzl * 16, nc), BF16),
            dma(4),
            dma(nka), dma(nka),
            dma(nzl), dma(nzl), dma(nzl), dma(nzl),
            dma(nzh), dma(nzh),
            dma(ny), dma(ny), dma(nx), dma(nx),
            dma(nx), dma(nx), dma(ny), dma(ny),
            dma(1), dma(1), dma(nzl), dma(nzl),
            dma(nka), dma(nka), dma(nx), dma(nx),
        ],
        compiler_params=pltpu.CompilerParams(
            collective_id=0, has_side_effects=True, vmem_limit_bytes=56 * 1024 * 1024
        ),
    )(
        q_table,
        exciton[0],
        orb_cond[0],
        orb_val.reshape(nx, 2, 16, nnu),
        screened.reshape(nka, nka, 32, nnu),
    )
    return out[None]


def build(mesh, nzh, factor):
    shape = mesh.shape
    sizes = (shape["ka"] // nzh, nzh, shape["row"], shape["col"] // 2)
    placed = (
        P("ka", None, None, None),
        P("ka", None, "row"),
        P("ka", None, "col"),
        P(None, "row", "col"),
        P(),
    )
    return jax.shard_map(
        functools.partial(local, sizes, factor),
        mesh=mesh, in_specs=placed, out_specs=P("ka", None, "col", None), check_vma=False,
    )


def solution(mesh):
    return build(mesh, NZH, math.sqrt(128 * 128) / 2048)
```

```python
import functools
import math

import jax
import jax.numpy as jnp
from jax import lax
from jax.experimental import pallas as pl
from jax.experimental.pallas import tpu as pltpu
from jax.sharding import PartitionSpec as P

NZH = 4
MESH = pl.DeviceIdType.MESH
BF16 = jnp.bfloat16
F32 = jnp.float32
NT = (((1,), (1,)), ((), ()))


def kernel(
    sizes, factor, q_ref, ex_hbm, cond_hbm, val_hbm, w_hbm, out_ref,
    ex_v, cond_v, condt, ct4, w_v, wf, psend, pb, vb, pairs, direct, hs, c1, tsum, zr, us, fr, xs,
    ld, p1s, p1r, p2s, p2r, pcs, pcr, v1s, v1r, vas, var, vbs, vbr, vcs, vcr, vds, vdr,
    h1s, h1r, h2s, h2r, h3s, h3r, h5s, h5r,
):
    ny, nzh, nx, nzl = sizes
    nka = ny * nzh
    rows, nv, nnu, nc = nzl * 32, nzl * 32, vb.shape[-1], condt.shape[-1]
    a, r, c = lax.axis_index("ka"), lax.axis_index("row"), lax.axis_index("col")
    y, zh = a // nzh, a % nzh
    zl, co = c // 2, c % 2
    partner = {"col": zl * 2 + 1 - co}
    near = sorted(range(nzh), key=lambda d: min(d, nzh - d))

    def at_ka(dy, dz):
        return {"ka": ((y + dy) % ny) * nzh + (zh + dz) % nzh}

    def at_zl(d):
        return {"col": ((zl + d) % nzl) * 2 + co}

    def at_row(d):
        return {"row": (r + d) % nx}

    def zof(d):
        return (zh + d) % nzh

    def send(src, dst, ss, rs, where):
        pltpu.make_async_remote_copy(
            src_ref=src, dst_ref=dst, send_sem=ss, recv_sem=rs, device_id=where, device_id_type=MESH
        ).start()

    def got(ref, rs):
        pltpu.make_async_copy(ref, ref, rs).wait()

    def each(lo, hi, body):
        def step(d, carry):
            body(d)
            return carry

        if hi > lo:
            lax.fori_loop(lo, hi, step, 0)

    load_ex = pltpu.make_async_copy(ex_hbm.at[zl], ex_v, ld.at[0])
    load_cond = pltpu.make_async_copy(cond_hbm, cond_v, ld.at[1])
    load_val = pltpu.make_async_copy(val_hbm.at[r], vb.at[zh, y, r], ld.at[2])
    load_w = pltpu.make_async_copy(w_hbm.at[:, a], w_v, ld.at[3])
    load_cond.start()
    load_ex.start()
    load_val.start()

    barrier = pltpu.get_barrier_semaphore()

    def hello(where):
        pl.semaphore_signal(barrier, inc=1, device_id=where, device_id_type=MESH)

    for dz in reversed(near):
        each(1 if dz == 0 else 0, ny, lambda dy: hello(at_ka(dy, dz)))
    each(1, nzl, lambda d: hello(at_zl(d)))
    each(1, nx, lambda d: hello(at_row(d)))
    hello(partner)
    load_w.start()

    load_cond.wait()
    condt[...] = cond_v[...].T.reshape(condt.shape)
    load_ex.wait()
    half_cond = condt[:, co].reshape(nka * 16, nc)
    psend[...] = (
        lax.dot_general(half_cond, ex_v[...], NT, preferred_element_type=F32)
        .astype(BF16)
        .reshape(psend.shape)
    )
    pb[zh, y, zl, co] = psend[a]
    load_val.wait()
    pl.semaphore_wait(barrier, nka + nzl + nx - 2)

    for dz in reversed(near):
        if dz:
            part = vb.at[zh, y, r]
            send(part, part, v1s.at[dz], v1r.at[(nzh - dz) % nzh], at_ka(0, dz))

    for dz in reversed(near):

        def p1(dy, dz=dz):
            to = ((y + dy) % ny) * nzh + zof(dz)
            send(
                psend.at[to], pb.at[zh, y, zl, co], p1s.at[dz, dy], p1r.at[(nzh - dz) % nzh],
                at_ka(dy, dz),
            )

        each(1 if dz == 0 else 0, ny, p1)

    load_w.wait()
    wf[...] = w_v[...].astype(F32)
    for k in range(nka):
        for b in range(nzl):
            ct4[k % nzh, k // nzh, b] = condt[k].reshape(32, nc)

    def first(d):
        zs = zof(d)
        if d:
            got(vb.at[zs, y, r], v1r.at[d])

        def v2a(e):
            part = vb.at[zs, y, r, 0]
            send(part, part, vas.at[d, e], var.at[d], at_ka(e, 0))

        def v2b(e):
            part = vb.at[zs, y, r, 1]
            send(part, part, vbs.at[d, e], vbr.at[d], at_row(e))

        each(1, ny, v2a)
        each(1, nx, v2b)
        have = ny if d else ny - 1
        if have:
            got(pb.at[zs, 0:have, zl, co], p1r.at[d])

        def p2(e):
            part = pb.at[zs, :, zl, co]
            send(part, part, p2s.at[d, e], p2r.at[d], at_zl(e))

        each(1, nzl, p2)

    def second(d):
        zs = zof(d)
        if ny > 1:
            got(vb.at[zs, 0 : ny - 1, r, 0], var.at[d])

        def v3a(e):
            part = vb.at[zs, :, r, 0]
            send(part, part, vcs.at[d, e], vcr.at[d], at_row(e))

        each(1, nx, v3a)
        if nx > 1:
            got(vb.at[zs, y, 0 : nx - 1, 1], vbr.at[d])

        def v3b(e):
            part = vb.at[zs, y, :, 1]
            send(part, part, vds.at[d, e], vdr.at[d], at_ka(e, 0))

        each(1, ny, v3b)
        if nzl > 1:
            got(pb.at[zs, :, 0 : nzl - 1, co], p2r.at[d])
        part = pb.at[zs, :, :, co]
        send(part, part, pcs.at[d], pcr.at[d], partner)

    def third(d):
        zs = zof(d)
        got(pb.at[zs, :, :, co], pcr.at[d])
        if nx > 1:
            got(vb.at[zs, :, 0 : nx - 1, 0], vcr.at[d])
        if ny > 1:
            got(vb.at[zs, 0 : ny - 1, :, 1], vdr.at[d])

        def pair(i, carry):
            panel = pb[zs, i].reshape(rows, nv)
            val = vb[zs, i].reshape(nv, nnu)
            pairs[zs, i] = jnp.dot(panel, val, preferred_element_type=F32).reshape(nzl, 32, nnu)
            return carry

        lax.fori_loop(0, ny, pair, 0)

    if nzh == 4:
        plan = (
            (first, 0), (first, 1), (first, 3), (second, 0), (first, 2), (second, 1),
            (second, 3), (third, 0), (second, 2), (third, 1), (third, 3), (third, 2),
        )
    else:
        plan = [(leg, d) for leg in (first, second, third) for d in near]
    for leg, d in plan:
        leg(d)

    lanes = nnu // 128

    def weigh(e):
        zk = zof(e)

        def tile(t, carry):
            s = pl.ds(pl.multiple_of((t // lanes) * 8, 8), 8)
            l = pl.ds(pl.multiple_of((t % lanes) * 128, 128), 128)
            sums = [[None] * nzl for _ in range(ny)]
            for z2 in range(nzh):
                for y2 in range(ny):
                    p = [pairs[z2, y2, b, s, l] for b in range(nzl)]
                    for i in range(ny):
                        w = wf[q_ref[y2 * nzh + z2, i * nzh + zk], s, l]
                        for b in range(nzl):
                            term = w * p[b]
                            sums[i][b] = term if sums[i][b] is None else sums[i][b] + term
            for i in range(ny):
                for b in range(nzl):
                    direct[i, b, s, l] = sums[i][b]
            return carry

        lax.fori_loop(0, 4 * lanes, tile, 0)

        def half(i, carry):
            d = direct[i].reshape(rows, nnu).astype(BF16)
            val = vb[zk, i].reshape(nv, nnu)
            h = lax.dot_general(val, d, NT, preferred_element_type=F32)
            hs[zk, i] = h.astype(BF16).reshape(nzl, 2, 16, rows)
            return carry

        lax.fori_loop(0, ny, half, 0)
        send(hs.at[zk, :, :, 1 - co], c1.at[zk], h1s.at[e], h1r.at[e], partner)

    def over_zl(e):
        zk = zof(e)
        got(c1.at[zk], h1r.at[e])

        def add_core(i, carry):
            tsum[zk, :, i] = (hs[zk, i, :, co].astype(F32) + c1[zk, i].astype(F32)).astype(BF16)
            return carry

        lax.fori_loop(0, ny, add_core, 0)

        def h2(d):
            send(
                tsum.at[zk, (zl + d) % nzl], zr.at[zk, d], h2s.at[e, d], h2r.at[e], at_zl(d)
            )

        each(1, nzl, h2)

    def over_ka(e):
        zk = zof(e)
        if nzl > 1:
            got(zr.at[zk, 0 : nzl - 1], h2r.at[e])

        def add_zl(i, carry):
            total = tsum[zk, zl, i].astype(F32)
            for d in range(1, nzl):
                total = total + zr[zk, d, i].astype(F32)
            us[zk, i] = total.astype(BF16)
            return carry

        lax.fori_loop(0, ny, add_zl, 0)

        def h3(dy):
            send(
                us.at[zk, (y + dy) % ny], fr.at[zh, y], h3s.at[e, dy], h3r.at[(nzh - e) % nzh],
                at_ka(dy, e),
            )

        each(1 if e == 0 else 0, ny, h3)
        if e == 0:
            fr[zh, y] = us[zh, y]

    far = near[::-1]
    for i, e in enumerate(far):
        weigh(e)
        if i:
            over_zl(far[i - 1])
    if nzh > 1:
        over_ka(far[0])
    over_zl(far[-1])
    for e in far[1:] if nzh > 1 else far:
        over_ka(e)

    lane_b = lax.broadcasted_iota(jnp.int32, (16, rows), 1) // 32
    total = jnp.zeros((nzl * 16, nc), F32)
    for d in near:
        have = ny if d else ny - 1
        zs = zof(d)
        if have:
            got(fr.at[zs, 0:have], h3r.at[d])
        for i in range(ny):
            f = fr[zs, i].astype(F32)
            lhs = jnp.concatenate(
                [jnp.where(lane_b == b, f, 0.0) for b in range(nzl)], axis=0
            ).astype(BF16)
            total = total + jnp.dot(
                lhs, ct4[zs, i].reshape(rows, nc), preferred_element_type=F32
            )
    xs[r] = total.astype(BF16)

    def h5(d):
        send(xs.at[r], xs.at[r], h5s.at[d], h5r.at[d], at_row(d))

    each(1, nx, h5)
    each(1, nx, lambda d: got(xs.at[r], h5r.at[d]))
    result = xs[0].astype(F32)
    for i in range(1, nx):
        result = result + xs[i].astype(F32)
    out_ref[...] = (result * factor).reshape(out_ref.shape)

    for d in range(nzh):
        if d:
            got(vb.at[zh, y, r], v1s.at[d])
        lo = 0 if d else 1
        each(lo, ny, lambda e: got(pb.at[zh, y, zl, co], p1s.at[d, e]))
        each(1, ny, lambda e: got(vb.at[zh, y, r, 0], vas.at[d, e]))
        each(1, nx, lambda e: got(vb.at[zh, y, r, 1], vbs.at[d, e]))
        each(1, nzl, lambda e: got(pb.at[zh, :, zl, co], p2s.at[d, e]))
        each(1, nx, lambda e: got(vb.at[zh, :, r, 0], vcs.at[d, e]))
        each(1, ny, lambda e: got(vb.at[zh, y, :, 1], vds.at[d, e]))
        got(pb.at[zh, :, :, co], pcs.at[d])
        got(c1.at[zh], h1s.at[d])
        each(1, nzl, lambda e: got(zr.at[zh, 0], h2s.at[d, e]))
        each(lo, ny, lambda e: got(fr.at[zh, y], h3s.at[d, e]))
    each(1, nx, lambda d: got(xs.at[r], h5s.at[d]))


def local(sizes, factor, exciton, orb_cond, orb_val, screened, q_table):
    ny, nzh, nx, nzl = sizes
    nka = ny * nzh
    nc = exciton.shape[-1]
    nv = nzl * 32
    rows = nzl * 32
    mu = nka * 32
    nnu = orb_val.shape[-1]
    any_space = pl.BlockSpec(memory_space=pl.ANY)
    dma = lambda *n: pltpu.SemaphoreType.DMA(n)
    vm = pltpu.VMEM
    out = pl.pallas_call(
        functools.partial(kernel, sizes, factor),
        name="isdf_direct",
        out_shape=jax.ShapeDtypeStruct((nzl, 16, nc), F32),
        in_specs=[pl.BlockSpec(memory_space=pltpu.SMEM)] + [any_space] * 4,
        out_specs=pl.BlockSpec(memory_space=pltpu.VMEM),
        scratch_shapes=[
            vm((nv, nc), BF16),
            vm((nc, mu), BF16),
            vm((nka, 2, 16, nc), BF16),
            vm((nzh, ny, nzl, 32, nc), BF16),
            vm((nka, 32, nnu), BF16),
            vm((nka, 32, nnu), F32),
            vm((nka, 16, nv), BF16),
            vm((nzh, ny, nzl, 2, 16, nv), BF16),
            vm((nzh, ny, nx, 2, 16, nnu), BF16),
            vm((nzh, ny, nzl, 32, nnu), F32),
            vm((ny, nzl, 32, nnu), F32),
            vm((nzh, ny, nzl, 2, 16, rows), BF16),
            vm((nzh, ny, nzl, 16, rows), BF16),
            vm((nzh, nzl, ny, 16, rows), BF16),
            vm((nzh, nzl, ny, 16, rows), BF16),
            vm((nzh, ny, 16, rows), BF16),
            vm((nzh, ny, 16, rows), BF16),
            vm((nx, nzl * 16, nc), BF16),
            dma(4),
            dma(nzh, ny), dma(nzh),
            dma(nzh, nzl), dma(nzh), dma(nzh), dma(nzh),
            dma(nzh), dma(nzh),
            dma(nzh, ny), dma(nzh), dma(nzh, nx), dma(nzh),
            dma(nzh, nx), dma(nzh), dma(nzh, ny), dma(nzh),
            dma(nzh), dma(nzh), dma(nzh, nzl), dma(nzh),
            dma(nzh, ny), dma(nzh), dma(nx), dma(nx),
        ],
        compiler_params=pltpu.CompilerParams(
            collective_id=0, has_side_effects=True, vmem_limit_bytes=56 * 1024 * 1024
        ),
    )(
        q_table,
        exciton[0],
        orb_cond[0],
        orb_val.reshape(nx, 2, 16, nnu),
        screened.reshape(nka, nka, 32, nnu),
    )
    return out[None]


def build(mesh, nzh, factor):
    shape = mesh.shape
    sizes = (shape["ka"] // nzh, nzh, shape["row"], shape["col"] // 2)
    placed = (
        P("ka", None, None, None),
        P("ka", None, "row"),
        P("ka", None, "col"),
        P(None, "row", "col"),
        P(),
    )
    return jax.shard_map(
        functools.partial(local, sizes, factor),
        mesh=mesh, in_specs=placed, out_specs=P("ka", None, "col", None), check_vma=False,
    )


def solution(mesh):
    return build(mesh, NZH, math.sqrt(128 * 128) / 2048)
```

```python
import functools
import math

import jax
import jax.numpy as jnp
from jax import lax
from jax.experimental import pallas as pl
from jax.experimental.pallas import tpu as pltpu
from jax.sharding import PartitionSpec as P

NZH = 4
MESH = pl.DeviceIdType.MESH
BF16 = jnp.bfloat16
F32 = jnp.float32
NT = (((1,), (1,)), ((), ()))


def kernel(
    sizes, factor, q_hbm, ex_hbm, cond_hbm, val_hbm, w_hbm, out_ref,
    q_ref, ex_v, cond_v, condt, ct4, w_v, wf, psend, prel, pb, vb, pairs, direct, hs, c1, tsum, zr, us, fr, xs,
    ld, p1s, p1r, prr, pfs, p2s, p2r, pcs, pcr, v1s, v1r, vxr, vfs, vgs, vys, vyr, vas, var, vbs, vbr, vcs, vcr, vds, vdr,
    h1s, h1r, h2s, h2r, h3s, h3r, h5s, h5r,
):
    ny, nzh, nx, nzl = sizes
    nka = ny * nzh
    rows, nv, nnu, nc = nzl * 32, nzl * 32, vb.shape[-1], condt.shape[-1]
    a, r, c = lax.axis_index("ka"), lax.axis_index("row"), lax.axis_index("col")
    y, zh = a // nzh, a % nzh
    zl, co = c // 2, c % 2
    partner = {"col": zl * 2 + 1 - co}
    near = sorted(range(nzh), key=lambda d: min(d, nzh - d))
    beside = [d for d in near if min(d, nzh - d) < 2]
    opposite = nzh > 2
    hy = ny // 2

    def at_ka(dy, dz):
        return {"ka": ((y + dy) % ny) * nzh + (zh + dz) % nzh}

    def at_zl(d):
        return {"col": ((zl + d) % nzl) * 2 + co}

    def at_row(d):
        return {"row": (r + d) % nx}

    def zof(d):
        return (zh + d) % nzh

    def send(src, dst, ss, rs, where):
        pltpu.make_async_remote_copy(
            src_ref=src, dst_ref=dst, send_sem=ss, recv_sem=rs, device_id=where, device_id_type=MESH
        ).start()

    def got(ref, rs):
        pltpu.make_async_copy(ref, ref, rs).wait()

    def each(lo, hi, body):
        def step(d, carry):
            body(d)
            return carry

        if hi > lo:
            lax.fori_loop(lo, hi, step, 0)

    load_ex = pltpu.make_async_copy(ex_hbm.at[zl], ex_v, ld.at[0])
    load_cond = pltpu.make_async_copy(cond_hbm, cond_v, ld.at[1])
    load_val = pltpu.make_async_copy(val_hbm.at[r], vb.at[zh, y, r], ld.at[2])
    load_w = pltpu.make_async_copy(w_hbm.at[:, a], w_v, ld.at[3])
    load_q = pltpu.make_async_copy(q_hbm, q_ref, ld.at[4])
    load_cond.start()
    load_ex.start()
    load_val.start()

    barrier = pltpu.get_barrier_semaphore()

    def hello(where):
        pl.semaphore_signal(barrier, inc=1, device_id=where, device_id_type=MESH)

    for dz in reversed(beside):
        each(1 if dz == 0 else 0, ny, lambda dy: hello(at_ka(dy, dz)))
    if opposite:

        @pl.when(zh < 2)
        def _():
            each(0, ny, lambda dy: hello(at_ka(dy, 2)))

    each(1, nzl, lambda d: hello(at_zl(d)))
    each(1, nx, lambda d: hello(at_row(d)))
    hello(partner)
    load_w.start()
    load_q.start()

    load_cond.wait()
    condt[...] = cond_v[...].T.reshape(condt.shape)
    load_ex.wait()
    half_cond = condt[:, co].reshape(nka * 16, nc)
    psend[...] = (
        lax.dot_general(half_cond, ex_v[...], NT, preferred_element_type=F32)
        .astype(BF16)
        .reshape(psend.shape)
    )
    pb[zh, y, zl, co] = psend[a]
    load_val.wait()
    greeted = ny * len(beside) + nzl + nx - 2
    if opposite:
        greeted = greeted + ny * (zh // 2)
    pl.semaphore_wait(barrier, greeted)

    if opposite:

        @pl.when(zh >= 2)
        def _():
            def p_far(dy):
                to = ((y + dy) % ny) * nzh + zof(2)
                send(psend.at[to], pb.at[zh, y, zl, co], p1s.at[2, dy], p1r.at[2], at_ka(dy, 2))

            each(0, ny, p_far)
            for u in range(2):
                part = vb.at[zh, y, r, u]
                send(part, part, vgs.at[u], vxr.at[u], at_ka(0, 2))

        @pl.when(zh < 2)
        def _():
            way = y // hy

            def p_far(dy):
                to_y = (y + dy) % ny
                send(
                    psend.at[to_y * nzh + zof(2)], prel.at[way, y % hy], p1s.at[2, dy],
                    prr.at[way], {"ka": to_y * nzh + zof(1 + (nzh - 2) * way)},
                )

            each(0, ny, p_far)

    for dz in beside[1:]:
        part = vb.at[zh, y, r]
        send(part, part, v1s.at[dz], v1r.at[(nzh - dz) % nzh], at_ka(0, dz))

    for dz in reversed(beside):

        def p1(dy, dz=dz):
            to = ((y + dy) % ny) * nzh + zof(dz)
            send(
                psend.at[to], pb.at[zh, y, zl, co], p1s.at[dz, dy], p1r.at[(nzh - dz) % nzh],
                at_ka(dy, dz),
            )

        each(1 if dz == 0 else 0, ny, p1)

    load_w.wait()
    load_q.wait()
    wf[...] = w_v[...].astype(F32)
    for k in range(nka):
        for b in range(nzl):
            ct4[k % nzh, k // nzh, b] = condt[k].reshape(32, nc)

    def relay(u):
        zs, on = zof(nzh - 1 + 2 * u), zof(nzh + 1 - 2 * u)
        got(vb.at[zs, y, r], v1r.at[(nzh - 1 + 2 * u) % nzh])
        part = vb.at[zs, y, r, u]
        send(part, part, vfs.at[0], vxr.at[u], {"ka": y * nzh + on})
        got(prel.at[u], prr.at[u])
        send(
            prel.at[u], pb.at[zs, pl.ds(u * hy, hy), zl, co], pfs.at[0], p1r.at[2],
            {"ka": y * nzh + on},
        )

    def first(d, far=False, own=False, relayed=False):
        zs = zof(d)
        if far:
            got(vb.at[zs, y, r, 0], vxr.at[0])
            got(vb.at[zs, y, r, 1], vxr.at[1])
        elif not (own or relayed):
            got(vb.at[zs, y, r], v1r.at[d])

        def v2a(e):
            part = vb.at[zs, y, r, 0]
            send(part, part, vas.at[d, e], var.at[d], at_ka(e, 0))

        def v2b(e):
            part = vb.at[zs, y, r, 1]
            send(part, part, vbs.at[d, e], vbr.at[d], at_row(e))

        def v_all(e):
            part = vb.at[zs, y, r]
            ex, ey = e // ny, e % ny
            where = {"ka": ((y + ey) % ny) * nzh + zh, "row": (r + ex) % nx}
            send(part, part, vys.at[ex, ey], vyr.at[ex, ey], where)

        if far:
            each(1, nx * ny, v_all)
        else:
            each(1, ny, v2a)
            each(1, nx, v2b)
        have = ny - 1 if own else ny
        if have:
            got(pb.at[zs, 0:have, zl, co], p1r.at[d])

        def p2(e):
            part = pb.at[zs, :, zl, co]
            send(part, part, p2s.at[d, e], p2r.at[d], at_zl(e))

        each(1, nzl, p2)

    def second_panels(d):
        zs = zof(d)
        if nzl > 1:
            got(pb.at[zs, :, 0 : nzl - 1, co], p2r.at[d])
        part = pb.at[zs, :, :, co]
        send(part, part, pcs.at[d], pcr.at[d], partner)

    def second(d):
        zs = zof(d)
        if ny > 1:
            got(vb.at[zs, 0 : ny - 1, r, 0], var.at[d])

        def v3a(e):
            part = vb.at[zs, :, r, 0]
            send(part, part, vcs.at[d, e], vcr.at[d], at_row(e))

        each(1, nx, v3a)
        if nx > 1:
            got(vb.at[zs, y, 0 : nx - 1, 1], vbr.at[d])

        def v3b(e):
            part = vb.at[zs, y, :, 1]
            send(part, part, vds.at[d, e], vdr.at[d], at_ka(e, 0))

        each(1, ny, v3b)
        second_panels(d)

    def third(d, far=False):
        zs = zof(d)
        got(pb.at[zs, :, :, co], pcr.at[d])
        if far:
            each(1, nx * ny, lambda e: got(vb.at[zs, y, r], vyr.at[e // ny, e % ny]))
        else:
            if nx > 1:
                got(vb.at[zs, :, 0 : nx - 1, 0], vcr.at[d])
            if ny > 1:
                got(vb.at[zs, 0 : ny - 1, :, 1], vdr.at[d])

        def pair(i, carry):
            panel = pb[zs, i].reshape(rows, nv)
            val = vb[zs, i].reshape(nv, nnu)
            pairs[zs, i] = jnp.dot(panel, val, preferred_element_type=F32).reshape(nzl, 32, nnu)
            return carry

        lax.fori_loop(0, ny, pair, 0)

    lanes = nnu // 128

    def weigh(e, sources, start=False):
        zk = zof(e)

        def tile(t, carry):
            s = pl.ds(pl.multiple_of(t * 8, 8), 8)
            blocks = [pl.ds(l * 128, 128) for l in range(lanes)]
            place = [(i, b, l) for i in range(ny) for b in range(nzl) for l in range(lanes)]
            sums = {
                (i, b, l): None if start else direct[zk, i, b, s, blocks[l]] for i, b, l in place
            }
            for d in sources:
                z2 = zof(d)
                for y2 in range(ny):
                    p = [[pairs[z2, y2, b, s, m] for m in blocks] for b in range(nzl)]
                    for i in range(ny):
                        q = q_ref[y2 * nzh + z2, i * nzh + zk]
                        for l in range(lanes):
                            w = wf[q, s, blocks[l]]
                            for b in range(nzl):
                                term = w * p[b][l]
                                old = sums[i, b, l]
                                sums[i, b, l] = term if old is None else old + term
            for i, b, l in place:
                direct[zk, i, b, s, blocks[l]] = sums[i, b, l]
            return carry

        lax.fori_loop(0, 4, tile, 0)

    def weigh_all(sources, start=False):
        def step(e, carry):
            weigh(e, sources, start)
            return carry

        lax.fori_loop(0, nzh, step, 0)

    if opposite:
        u0 = ((zh + 1) // 2 + 1) % 2
        u1 = 1 - u0
        d0, d1 = (nzh - 1 + 2 * u0) % nzh, (nzh - 1 + 2 * u1) % nzh
        relay(u0)
        first(d0, relayed=True)
        first(0, own=True)
        first(d1)
        second(d0)
        second(0)
        first(2, far=True)
        second(d1)
        third(d0)
        second_panels(2)
        third(0)
        weigh_all((d0, 0), start=True)
        third(d1)
        third(2, far=True)
        late = (d1, 2)
    else:
        for d in near:
            first(d, own=d == 0)
        for d in near:
            second(d)
        third(0)
        weigh_all((0,), start=True)
        for d in near[1:]:
            third(d)
        late = tuple(near[1:])

    def halves(e):
        zk = zof(e)

        def half(i, carry):
            d = direct[zk, i].reshape(rows, nnu).astype(BF16)
            val = vb[zk, i].reshape(nv, nnu)
            h = lax.dot_general(val, d, NT, preferred_element_type=F32)
            hs[zk, i] = h.astype(BF16).reshape(nzl, 2, 16, rows)
            return carry

        lax.fori_loop(0, ny, half, 0)
        send(hs.at[zk, :, :, 1 - co], c1.at[zk], h1s.at[e], h1r.at[e], partner)

    def over_zl(e):
        zk = zof(e)
        got(c1.at[zk], h1r.at[e])

        def add_core(i, carry):
            tsum[zk, :, i] = (hs[zk, i, :, co].astype(F32) + c1[zk, i].astype(F32)).astype(BF16)
            return carry

        lax.fori_loop(0, ny, add_core, 0)

        def h2(d):
            send(
                tsum.at[zk, (zl + d) % nzl], zr.at[zk, d], h2s.at[e, d], h2r.at[e], at_zl(d)
            )

        each(1, nzl, h2)

    def over_ka(e):
        zk = zof(e)
        if nzl > 1:
            got(zr.at[zk, 0 : nzl - 1], h2r.at[e])

        def add_zl(i, carry):
            total = tsum[zk, zl, i].astype(F32)
            for d in range(1, nzl):
                total = total + zr[zk, d, i].astype(F32)
            us[zk, i] = total.astype(BF16)
            return carry

        lax.fori_loop(0, ny, add_zl, 0)

        def h3(dy):
            send(
                us.at[zk, (y + dy) % ny], fr.at[zh, y], h3s.at[e, dy], h3r.at[(nzh - e) % nzh],
                at_ka(dy, e),
            )

        each(1 if e == 0 else 0, ny, h3)
        if e == 0:
            fr[zh, y] = us[zh, y]

    far = near[::-1]
    for i, e in enumerate(far):
        if late:
            weigh(e, late)
        halves(e)
        if i:
            over_zl(far[i - 1])
    over_zl(far[-1])
    for e in far:
        over_ka(e)

    lane_b = lax.broadcasted_iota(jnp.int32, (16, rows), 1) // 32
    total = jnp.zeros((nzl * 16, nc), F32)
    for d in near[1:] + near[:1]:
        have = ny if d else ny - 1
        zs = zof(d)
        if have:
            got(fr.at[zs, 0:have], h3r.at[d])
        for i in range(ny):
            f = fr[zs, i].astype(F32)
            lhs = jnp.concatenate(
                [jnp.where(lane_b == b, f, 0.0) for b in range(nzl)], axis=0
            ).astype(BF16)
            total = total + jnp.dot(
                lhs, ct4[zs, i].reshape(rows, nc), preferred_element_type=F32
            )
    xs[r] = total.astype(BF16)

    def h5(d):
        send(xs.at[r], xs.at[r], h5s.at[d], h5r.at[d], at_row(d))

    each(1, nx, h5)

    for d in range(nzh):
        lo = 0 if d else 1
        if d in beside[1:]:
            got(vb.at[zh, y, r], v1s.at[d])
        each(lo, ny, lambda e: got(pb.at[zh, y, zl, co], p1s.at[d, e]))
        if d == 2 and opposite:
            each(1, nx * ny, lambda e: got(vb.at[zh, y, r], vys.at[e // ny, e % ny]))
        else:
            each(1, ny, lambda e: got(vb.at[zh, y, r, 0], vas.at[d, e]))
            each(1, nx, lambda e: got(vb.at[zh, y, r, 1], vbs.at[d, e]))
        each(1, nzl, lambda e: got(pb.at[zh, :, zl, co], p2s.at[d, e]))
        if d != 2 or not opposite:
            each(1, nx, lambda e: got(vb.at[zh, :, r, 0], vcs.at[d, e]))
            each(1, ny, lambda e: got(vb.at[zh, y, :, 1], vds.at[d, e]))
        got(pb.at[zh, :, :, co], pcs.at[d])
        got(c1.at[zh], h1s.at[d])
        each(1, nzl, lambda e: got(zr.at[zh, 0], h2s.at[d, e]))
        each(lo, ny, lambda e: got(fr.at[zh, y], h3s.at[d, e]))
    if opposite:
        got(vb.at[zh, y, r, 0], vfs.at[0])
        got(prel.at[0], pfs.at[0])

        @pl.when(zh >= 2)
        def _():
            for u in range(2):
                got(vb.at[zh, y, r, u], vgs.at[u])

    each(1, nx, lambda d: got(xs.at[r], h5r.at[d]))
    result = xs[0].astype(F32)
    for i in range(1, nx):
        result = result + xs[i].astype(F32)
    out_ref[...] = (result * factor).reshape(out_ref.shape)

    each(1, nx, lambda d: got(xs.at[r], h5s.at[d]))


def local(sizes, factor, exciton, orb_cond, orb_val, screened, q_table):
    ny, nzh, nx, nzl = sizes
    nka = ny * nzh
    nc = exciton.shape[-1]
    nv = nzl * 32
    rows = nzl * 32
    mu = nka * 32
    nnu = orb_val.shape[-1]
    any_space = pl.BlockSpec(memory_space=pl.ANY)
    dma = lambda *n: pltpu.SemaphoreType.DMA(n)
    vm = pltpu.VMEM
    out = pl.pallas_call(
        functools.partial(kernel, sizes, factor),
        name="isdf_direct",
        out_shape=jax.ShapeDtypeStruct((nzl, 16, nc), F32),
        in_specs=[any_space] * 5,
        out_specs=pl.BlockSpec(memory_space=pltpu.VMEM),
        scratch_shapes=[
            pltpu.SMEM((nka, nka), jnp.int32),
            vm((nv, nc), BF16),
            vm((nc, mu), BF16),
            vm((nka, 2, 16, nc), BF16),
            vm((nzh, ny, nzl, 32, nc), BF16),
            vm((nka, 32, nnu), BF16),
            vm((nka, 32, nnu), F32),
            vm((nka, 16, nv), BF16),
            vm((2, max(1, ny // 2), 16, nv), BF16),
            vm((nzh, ny, nzl, 2, 16, nv), BF16),
            vm((nzh, ny, nx, 2, 16, nnu), BF16),
            vm((nzh, ny, nzl, 32, nnu), F32),
            vm((nzh, ny, nzl, 32, nnu), F32),
            vm((nzh, ny, nzl, 2, 16, rows), BF16),
            vm((nzh, ny, nzl, 16, rows), BF16),
            vm((nzh, nzl, ny, 16, rows), BF16),
            vm((nzh, nzl, ny, 16, rows), BF16),
            vm((nzh, ny, 16, rows), BF16),
            vm((nzh, ny, 16, rows), BF16),
            vm((nx, nzl * 16, nc), BF16),
            dma(5),
            dma(nzh, ny), dma(nzh), dma(2), dma(1),
            dma(nzh, nzl), dma(nzh), dma(nzh), dma(nzh),
            dma(nzh), dma(nzh), dma(2), dma(1), dma(2), dma(nx, ny), dma(nx, ny),
            dma(nzh, ny), dma(nzh), dma(nzh, nx), dma(nzh),
            dma(nzh, nx), dma(nzh), dma(nzh, ny), dma(nzh),
            dma(nzh), dma(nzh), dma(nzh, nzl), dma(nzh),
            dma(nzh, ny), dma(nzh), dma(nx), dma(nx),
        ],
        compiler_params=pltpu.CompilerParams(
            collective_id=0, has_side_effects=True, vmem_limit_bytes=56 * 1024 * 1024
        ),
    )(
        q_table,
        exciton[0],
        orb_cond[0],
        orb_val.reshape(nx, 2, 16, nnu),
        screened.reshape(nka, nka, 32, nnu),
    )
    return out[None]


def build(mesh, nzh, factor):
    shape = mesh.shape
    sizes = (shape["ka"] // nzh, nzh, shape["row"], shape["col"] // 2)
    placed = (
        P("ka", None, None, None),
        P("ka", None, "row"),
        P("ka", None, "col"),
        P(None, "row", "col"),
        P(),
    )
    return jax.shard_map(
        functools.partial(local, sizes, factor),
        mesh=mesh, in_specs=placed, out_specs=P("ka", None, "col", None), check_vma=False,
    )


def solution(mesh):
    return build(mesh, NZH, math.sqrt(128 * 128) / 2048)
```

```python
import functools
import math

import jax
import jax.numpy as jnp
from jax import lax
from jax.experimental import pallas as pl
from jax.experimental.pallas import tpu as pltpu
from jax.sharding import PartitionSpec as P

NZH = 4
MESH = pl.DeviceIdType.MESH
BF16 = jnp.bfloat16
F32 = jnp.float32
NT = (((1,), (1,)), ((), ()))


def kernel(
    sizes, factor, q_hbm, ex_hbm, cond_hbm, val_hbm, w_hbm, out_ref,
    q_ref, ex_v, cond_v, condt, ct4, w_v, wf, psend, powns, prel, pb, vb, pairs, direct, hs, c1, tsum, zr, us, fr, xs,
    ld, p1s, p1r, prr, pfs, p2s, p2r, pcs, pcr, v1s, v1r, vxr, vfs, vgs, vys, vyr, vas, var, vbs, vbr, vcs, vcr, vds, vdr,
    h1s, h1r, h2s, h2r, h3s, h3r, h5s, h5r,
):
    ny, nzh, nx, nzl = sizes
    nka = ny * nzh
    rows, nv, nnu, nc = nzl * 32, nzl * 32, vb.shape[-1], condt.shape[-1]
    a, r, c = lax.axis_index("ka"), lax.axis_index("row"), lax.axis_index("col")
    y, zh = a // nzh, a % nzh
    zl, co = c // 2, c % 2
    partner = {"col": zl * 2 + 1 - co}
    near = sorted(range(nzh), key=lambda d: min(d, nzh - d))
    beside = [d for d in near if min(d, nzh - d) < 2]
    opposite = nzh > 2
    hy = ny // 2

    def at_ka(dy, dz):
        return {"ka": ((y + dy) % ny) * nzh + (zh + dz) % nzh}

    def at_zl(d):
        return {"col": ((zl + d) % nzl) * 2 + co}

    def at_row(d):
        return {"row": (r + d) % nx}

    def zof(d):
        return (zh + d) % nzh

    def send(src, dst, ss, rs, where):
        pltpu.make_async_remote_copy(
            src_ref=src, dst_ref=dst, send_sem=ss, recv_sem=rs, device_id=where, device_id_type=MESH
        ).start()

    def got(ref, rs):
        pltpu.make_async_copy(ref, ref, rs).wait()

    def each(lo, hi, body):
        def step(d, carry):
            body(d)
            return carry

        if hi > lo:
            lax.fori_loop(lo, hi, step, 0)

    load_ex = pltpu.make_async_copy(ex_hbm, ex_v, ld.at[0])
    load_cond = pltpu.make_async_copy(cond_hbm, cond_v, ld.at[1])
    load_val = pltpu.make_async_copy(val_hbm.at[r], vb.at[zh, y, r], ld.at[2])
    load_w = pltpu.make_async_copy(w_hbm.at[:, a], w_v, ld.at[3])
    load_q = pltpu.make_async_copy(q_hbm, q_ref, ld.at[4])
    load_cond.start()
    load_ex.start()
    load_val.start()

    barrier = pltpu.get_barrier_semaphore()

    def hello(where):
        pl.semaphore_signal(barrier, inc=1, device_id=where, device_id_type=MESH)

    for dz in reversed(beside):
        each(1 if dz == 0 else 0, ny, lambda dy: hello(at_ka(dy, dz)))
    if opposite:

        @pl.when(zh < 2)
        def _():
            each(0, ny, lambda dy: hello(at_ka(dy, 2)))

    each(1, nzl, lambda d: hello(at_zl(d)))
    each(1, nx, lambda d: hello(at_row(d)))
    hello(partner)
    load_w.start()
    load_q.start()

    load_cond.wait()
    condt[...] = cond_v[...].T.reshape(condt.shape)
    load_ex.wait()
    half_cond = condt[:, co].reshape(nka * 16, nc)
    psend[...] = (
        lax.dot_general(half_cond, ex_v[zl], NT, preferred_element_type=F32)
        .astype(BF16)
        .reshape(psend.shape)
    )
    own_cond = jnp.concatenate([condt[i * nzh + zh].reshape(32, nc) for i in range(ny)], axis=0)
    for b in range(nzl):
        own = lax.dot_general(own_cond, ex_v[b], NT, preferred_element_type=F32)
        powns[:, b] = own.astype(BF16).reshape(ny, 2, 16, nv)
    pb[zh, y] = powns[y]
    load_val.wait()
    greeted = ny * len(beside) + nzl + nx - 2
    if opposite:
        greeted = greeted + ny * (zh // 2)
    pl.semaphore_wait(barrier, greeted)

    if opposite:

        @pl.when(zh >= 2)
        def _():
            def p_far(dy):
                to = ((y + dy) % ny) * nzh + zof(2)
                send(psend.at[to], pb.at[zh, y, zl, co], p1s.at[2, dy], p1r.at[2], at_ka(dy, 2))

            each(0, ny, p_far)
            for u in range(2):
                part = vb.at[zh, y, r, u]
                send(part, part, vgs.at[u], vxr.at[u], at_ka(0, 2))

        @pl.when(zh < 2)
        def _():
            way = y // hy

            def p_far(dy):
                to_y = (y + dy) % ny
                send(
                    psend.at[to_y * nzh + zof(2)], prel.at[way, y % hy], p1s.at[2, dy],
                    prr.at[way], {"ka": to_y * nzh + zof(1 + (nzh - 2) * way)},
                )

            each(0, ny, p_far)

    for dz in beside[1:]:
        part = vb.at[zh, y, r]
        send(part, part, v1s.at[dz], v1r.at[(nzh - dz) % nzh], at_ka(0, dz))

    for dz in reversed(beside[1:]):

        def p1(dy, dz=dz):
            to = ((y + dy) % ny) * nzh + zof(dz)
            send(
                psend.at[to], pb.at[zh, y, zl, co], p1s.at[dz, dy], p1r.at[(nzh - dz) % nzh],
                at_ka(dy, dz),
            )

        each(0, ny, p1)

    def p_own(dy):
        send(powns.at[(y + dy) % ny], pb.at[zh, y], p1s.at[0, dy], p1r.at[0], at_ka(dy, 0))

    each(1, ny, p_own)

    def relay(u):
        zs, on = zof(nzh - 1 + 2 * u), zof(nzh + 1 - 2 * u)
        got(vb.at[zs, y, r], v1r.at[(nzh - 1 + 2 * u) % nzh])
        part = vb.at[zs, y, r, u]
        send(part, part, vfs.at[0], vxr.at[u], {"ka": y * nzh + on})
        got(prel.at[u], prr.at[u])
        send(
            prel.at[u], pb.at[zs, pl.ds(u * hy, hy), zl, co], pfs.at[0], p1r.at[2],
            {"ka": y * nzh + on},
        )

    def first(d, far=False, own=False, relayed=False):
        zs = zof(d)
        if far:
            got(vb.at[zs, y, r, 0], vxr.at[0])
            got(vb.at[zs, y, r, 1], vxr.at[1])
        elif not (own or relayed):
            got(vb.at[zs, y, r], v1r.at[d])

        def v2a(e):
            part = vb.at[zs, y, r, 0]
            send(part, part, vas.at[d, e], var.at[d], at_ka(e, 0))

        def v2b(e):
            part = vb.at[zs, y, r, 1]
            send(part, part, vbs.at[d, e], vbr.at[d], at_row(e))

        def v_all(e):
            part = vb.at[zs, y, r]
            ex, ey = e // ny, e % ny
            where = {"ka": ((y + ey) % ny) * nzh + zh, "row": (r + ex) % nx}
            send(part, part, vys.at[ex, ey], vyr.at[ex, ey], where)

        if far:
            each(1, nx * ny, v_all)
        else:
            each(1, ny, v2a)
            each(1, nx, v2b)
        if own:
            return
        got(pb.at[zs, :, zl, co], p1r.at[d])

        def p2(e):
            part = pb.at[zs, :, zl, co]
            send(part, part, p2s.at[d, e], p2r.at[d], at_zl(e))

        each(1, nzl, p2)

    def second_panels(d):
        zs = zof(d)
        if nzl > 1:
            got(pb.at[zs, :, 0 : nzl - 1, co], p2r.at[d])
        part = pb.at[zs, :, :, co]
        send(part, part, pcs.at[d], pcr.at[d], partner)

    def second(d, own=False):
        zs = zof(d)
        if ny > 1:
            got(vb.at[zs, 0 : ny - 1, r, 0], var.at[d])

        def v3a(e):
            part = vb.at[zs, :, r, 0]
            send(part, part, vcs.at[d, e], vcr.at[d], at_row(e))

        each(1, nx, v3a)
        if nx > 1:
            got(vb.at[zs, y, 0 : nx - 1, 1], vbr.at[d])

        def v3b(e):
            part = vb.at[zs, y, :, 1]
            send(part, part, vds.at[d, e], vdr.at[d], at_ka(e, 0))

        each(1, ny, v3b)
        if not own:
            second_panels(d)

    def third(d, far=False, own=False):
        zs = zof(d)
        if not own:
            got(pb.at[zs, :, :, co], pcr.at[d])
        elif ny > 1:
            got(pb.at[zs, 0 : ny - 1], p1r.at[0])
        if far:
            each(1, nx * ny, lambda e: got(vb.at[zs, y, r], vyr.at[e // ny, e % ny]))
        else:
            if nx > 1:
                got(vb.at[zs, :, 0 : nx - 1, 0], vcr.at[d])
            if ny > 1:
                got(vb.at[zs, 0 : ny - 1, :, 1], vdr.at[d])

        for i in range(ny):
            panel = pb[zs, i].reshape(rows, nv)
            val = vb[zs, i].reshape(nv, nnu)
            pairs[zs, i] = jnp.dot(panel, val, preferred_element_type=F32).reshape(nzl, 32, nnu)

    lanes = nnu // 128

    def weigh(e, sources, start=False):
        zk = zof(e)

        def tile(t, carry):
            s = pl.ds(pl.multiple_of(t * 8, 8), 8)
            blocks = [pl.ds(l * 128, 128) for l in range(lanes)]
            place = [(i, b, l) for i in range(ny) for b in range(nzl) for l in range(lanes)]
            sums = {
                (i, b, l): None if start else direct[zk, i, b, s, blocks[l]] for i, b, l in place
            }
            for d in sources:
                z2 = zof(d)
                for y2 in range(ny):
                    p = [[pairs[z2, y2, b, s, m] for m in blocks] for b in range(nzl)]
                    for i in range(ny):
                        q = q_ref[y2 * nzh + z2, i * nzh + zk]
                        for l in range(lanes):
                            w = wf[q, s, blocks[l]]
                            for b in range(nzl):
                                term = w * p[b][l]
                                old = sums[i, b, l]
                                sums[i, b, l] = term if old is None else old + term
            for i, b, l in place:
                direct[zk, i, b, s, blocks[l]] = sums[i, b, l]
            return carry

        lax.fori_loop(0, 4, tile, 0)

    def weigh_all(sources, lo, hi, start=False):
        def step(e, carry):
            weigh(e, sources, start)
            return carry

        lax.fori_loop(lo, hi, step, 0)

    first(0, own=True)
    load_w.wait()
    load_q.wait()
    wf[...] = w_v[...].astype(F32)
    for k in range(nka):
        for b in range(nzl):
            ct4[k % nzh, k // nzh, b] = condt[k].reshape(32, nc)

    if opposite:
        u0 = ((zh + 1) // 2 + 1) % 2
        u1 = 1 - u0
        d0, d1 = (nzh - 1 + 2 * u0) % nzh, (nzh - 1 + 2 * u1) % nzh
        second(0, own=True)
        relay(u0)
        first(d0, relayed=True)
        first(d1)
        third(0, own=True)
        weigh_all((0,), 0, nzh, True)
        second(d0)
        first(2, far=True)
        second(d1)
        third(d0)
        before = nzh * (1 - zh // 2)
        weigh_all((d0,), 0, before)
        second_panels(2)
        weigh_all((d0,), before, nzh)
        third(d1)
        third(2, far=True)
        late = (d1, 2)
    else:
        for d in near[1:]:
            first(d)
        for d in near:
            second(d, own=d == 0)
        third(0, own=True)
        weigh_all((0,), 0, nzh, True)
        for d in near[1:]:
            third(d)
        late = tuple(near[1:])

    def halves(e):
        zk = zof(e)

        for i in range(ny):
            d = direct[zk, i].reshape(rows, nnu).astype(BF16)
            val = vb[zk, i].reshape(nv, nnu)
            h = lax.dot_general(val, d, NT, preferred_element_type=F32)
            hs[zk, i] = h.astype(BF16).reshape(nzl, 2, 16, rows)
        send(hs.at[zk, :, :, 1 - co], c1.at[zk], h1s.at[e], h1r.at[e], partner)

    def over_zl(e):
        zk = zof(e)
        got(c1.at[zk], h1r.at[e])

        def add_core(i, carry):
            tsum[zk, :, i] = (hs[zk, i, :, co].astype(F32) + c1[zk, i].astype(F32)).astype(BF16)
            return carry

        lax.fori_loop(0, ny, add_core, 0)

        def h2(d):
            send(
                tsum.at[zk, (zl + d) % nzl], zr.at[zk, d], h2s.at[e, d], h2r.at[e], at_zl(d)
            )

        each(1, nzl, h2)

    def over_ka(e):
        zk = zof(e)
        if nzl > 1:
            got(zr.at[zk, 0 : nzl - 1], h2r.at[e])

        def add_zl(i, carry):
            total = tsum[zk, zl, i].astype(F32)
            for d in range(1, nzl):
                total = total + zr[zk, d, i].astype(F32)
            us[zk, i] = total.astype(BF16)
            return carry

        lax.fori_loop(0, ny, add_zl, 0)

        def h3(dy):
            send(
                us.at[zk, (y + dy) % ny], fr.at[zh, y], h3s.at[e, dy], h3r.at[(nzh - e) % nzh],
                at_ka(dy, e),
            )

        each(1 if e == 0 else 0, ny, h3)
        if e == 0:
            fr[zh, y] = us[zh, y]

    far = near[::-1]
    for i, e in enumerate(far):
        if late:
            weigh(e, late)
        halves(e)
        if i:
            over_zl(far[i - 1])
    over_zl(far[-1])
    for e in far:
        over_ka(e)

    lane_b = lax.broadcasted_iota(jnp.int32, (16, rows), 1) // 32
    total = jnp.zeros((nzl * 16, nc), F32)
    for d in near[1:] + near[:1]:
        have = ny if d else ny - 1
        zs = zof(d)
        if have:
            got(fr.at[zs, 0:have], h3r.at[d])
        for i in range(ny):
            f = fr[zs, i].astype(F32)
            lhs = jnp.concatenate(
                [jnp.where(lane_b == b, f, 0.0) for b in range(nzl)], axis=0
            ).astype(BF16)
            total = total + jnp.dot(
                lhs, ct4[zs, i].reshape(rows, nc), preferred_element_type=F32
            )
    xs[r] = total.astype(BF16)

    def h5(d):
        send(xs.at[r], xs.at[r], h5s.at[d], h5r.at[d], at_row(d))

    each(1, nx, h5)

    for d in range(nzh):
        if d in beside[1:]:
            got(vb.at[zh, y, r], v1s.at[d])
        if d == 0:
            each(1, ny, lambda e: got(pb.at[zh, y], p1s.at[d, e]))
        else:
            each(0, ny, lambda e: got(pb.at[zh, y, zl, co], p1s.at[d, e]))
            each(1, nzl, lambda e: got(pb.at[zh, :, zl, co], p2s.at[d, e]))
            got(pb.at[zh, :, :, co], pcs.at[d])
        if d == 2 and opposite:
            each(1, nx * ny, lambda e: got(vb.at[zh, y, r], vys.at[e // ny, e % ny]))
        else:
            each(1, ny, lambda e: got(vb.at[zh, y, r, 0], vas.at[d, e]))
            each(1, nx, lambda e: got(vb.at[zh, y, r, 1], vbs.at[d, e]))
        if d != 2 or not opposite:
            each(1, nx, lambda e: got(vb.at[zh, :, r, 0], vcs.at[d, e]))
            each(1, ny, lambda e: got(vb.at[zh, y, :, 1], vds.at[d, e]))
        got(c1.at[zh], h1s.at[d])
        each(1, nzl, lambda e: got(zr.at[zh, 0], h2s.at[d, e]))
        each(0 if d else 1, ny, lambda e: got(fr.at[zh, y], h3s.at[d, e]))
    if opposite:
        got(vb.at[zh, y, r, 0], vfs.at[0])
        got(prel.at[0], pfs.at[0])

        @pl.when(zh >= 2)
        def _():
            for u in range(2):
                got(vb.at[zh, y, r, u], vgs.at[u])

    each(1, nx, lambda d: got(xs.at[r], h5r.at[d]))
    result = xs[0].astype(F32)
    for i in range(1, nx):
        result = result + xs[i].astype(F32)
    out_ref[...] = (result * factor).reshape(out_ref.shape)

    each(1, nx, lambda d: got(xs.at[r], h5s.at[d]))


def local(sizes, factor, exciton, orb_cond, orb_val, screened, q_table):
    ny, nzh, nx, nzl = sizes
    nka = ny * nzh
    nc = exciton.shape[-1]
    nv = nzl * 32
    rows = nzl * 32
    mu = nka * 32
    nnu = orb_val.shape[-1]
    any_space = pl.BlockSpec(memory_space=pl.ANY)
    dma = lambda *n: pltpu.SemaphoreType.DMA(n)
    vm = pltpu.VMEM
    out = pl.pallas_call(
        functools.partial(kernel, sizes, factor),
        name="isdf_direct",
        out_shape=jax.ShapeDtypeStruct((nzl, 16, nc), F32),
        in_specs=[any_space] * 5,
        out_specs=pl.BlockSpec(memory_space=pltpu.VMEM),
        scratch_shapes=[
            pltpu.SMEM((nka, nka), jnp.int32),
            vm((nzl, nv, nc), BF16),
            vm((nc, mu), BF16),
            vm((nka, 2, 16, nc), BF16),
            vm((nzh, ny, nzl, 32, nc), BF16),
            vm((nka, 32, nnu), BF16),
            vm((nka, 32, nnu), F32),
            vm((nka, 16, nv), BF16),
            vm((ny, nzl, 2, 16, nv), BF16),
            vm((2, max(1, ny // 2), 16, nv), BF16),
            vm((nzh, ny, nzl, 2, 16, nv), BF16),
            vm((nzh, ny, nx, 2, 16, nnu), BF16),
            vm((nzh, ny, nzl, 32, nnu), F32),
            vm((nzh, ny, nzl, 32, nnu), F32),
            vm((nzh, ny, nzl, 2, 16, rows), BF16),
            vm((nzh, ny, nzl, 16, rows), BF16),
            vm((nzh, nzl, ny, 16, rows), BF16),
            vm((nzh, nzl, ny, 16, rows), BF16),
            vm((nzh, ny, 16, rows), BF16),
            vm((nzh, ny, 16, rows), BF16),
            vm((nx, nzl * 16, nc), BF16),
            dma(5),
            dma(nzh, ny), dma(nzh), dma(2), dma(1),
            dma(nzh, nzl), dma(nzh), dma(nzh), dma(nzh),
            dma(nzh), dma(nzh), dma(2), dma(1), dma(2), dma(nx, ny), dma(nx, ny),
            dma(nzh, ny), dma(nzh), dma(nzh, nx), dma(nzh),
            dma(nzh, nx), dma(nzh), dma(nzh, ny), dma(nzh),
            dma(nzh), dma(nzh), dma(nzh, nzl), dma(nzh),
            dma(nzh, ny), dma(nzh), dma(nx), dma(nx),
        ],
        compiler_params=pltpu.CompilerParams(
            collective_id=0, has_side_effects=True, vmem_limit_bytes=56 * 1024 * 1024
        ),
    )(
        q_table,
        exciton[0],
        orb_cond[0],
        orb_val.reshape(nx, 2, 16, nnu),
        screened.reshape(nka, nka, 32, nnu),
    )
    return out[None]


def build(mesh, nzh, factor):
    shape = mesh.shape
    sizes = (shape["ka"] // nzh, nzh, shape["row"], shape["col"] // 2)
    placed = (
        P("ka", None, None, None),
        P("ka", None, "row"),
        P("ka", None, "col"),
        P(None, "row", "col"),
        P(),
    )
    return jax.shard_map(
        functools.partial(local, sizes, factor),
        mesh=mesh, in_specs=placed, out_specs=P("ka", None, "col", None), check_vma=False,
    )


def solution(mesh):
    return build(mesh, NZH, math.sqrt(128 * 128) / 2048)
```

```python
import functools
import math

import jax
import jax.numpy as jnp
from jax import lax
from jax.experimental import pallas as pl
from jax.experimental.pallas import tpu as pltpu
from jax.sharding import PartitionSpec as P

NZH = 4
MESH = pl.DeviceIdType.MESH
BF16 = jnp.bfloat16
F32 = jnp.float32
NT = (((1,), (1,)), ((), ()))


def kernel(
    sizes, factor, q_hbm, ex_hbm, cond_hbm, val_hbm, w_hbm, out_ref,
    q_ref, ex_v, cond_v, condt, ct4, w_v, wf, psend, powns, prel, pb, vb, pairs, direct, hs, c1, tsum, zr, us, fr, xs,
    ld, p1s, p1r, prr, pfs, p2s, p2r, pcs, pcr, v1s, v1r, vxr, vfs, vgs, vys, vyr, vas, var, vbs, vbr, vcs, vcr, vds, vdr,
    h1s, h1r, h2s, h2r, h3s, h3r, h5s, h5r,
):
    ny, nzh, nx, nzl = sizes
    nka = ny * nzh
    rows, nv, nnu, nc = nzl * 32, nzl * 32, vb.shape[-1], condt.shape[-1]
    a, r, c = lax.axis_index("ka"), lax.axis_index("row"), lax.axis_index("col")
    y, zh = a // nzh, a % nzh
    zl, co = c // 2, c % 2
    partner = {"col": zl * 2 + 1 - co}
    near = sorted(range(nzh), key=lambda d: min(d, nzh - d))
    beside = [d for d in near if min(d, nzh - d) < 2]
    opposite = nzh > 2
    hy = ny // 2

    def at_ka(dy, dz):
        return {"ka": ((y + dy) % ny) * nzh + (zh + dz) % nzh}

    def at_zl(d):
        return {"col": ((zl + d) % nzl) * 2 + co}

    def at_row(d):
        return {"row": (r + d) % nx}

    def zof(d):
        return (zh + d) % nzh

    def send(src, dst, ss, rs, where):
        pltpu.make_async_remote_copy(
            src_ref=src, dst_ref=dst, send_sem=ss, recv_sem=rs, device_id=where, device_id_type=MESH
        ).start()

    def got(ref, rs):
        pltpu.make_async_copy(ref, ref, rs).wait()

    def each(lo, hi, body):
        def step(d, carry):
            body(d)
            return carry

        if hi > lo:
            lax.fori_loop(lo, hi, step, 0)

    load_ex = pltpu.make_async_copy(ex_hbm, ex_v, ld.at[0])
    load_cond = pltpu.make_async_copy(cond_hbm, cond_v, ld.at[1])
    load_val = pltpu.make_async_copy(val_hbm.at[r], vb.at[zh, y, r], ld.at[2])
    load_w = pltpu.make_async_copy(w_hbm.at[:, a], w_v, ld.at[3])
    load_q = pltpu.make_async_copy(q_hbm, q_ref, ld.at[4])
    load_cond.start()
    load_ex.start()
    load_val.start()

    barrier = pltpu.get_barrier_semaphore()

    def hello(where):
        pl.semaphore_signal(barrier, inc=1, device_id=where, device_id_type=MESH)

    for dz in reversed(beside):
        each(1 if dz == 0 else 0, ny, lambda dy: hello(at_ka(dy, dz)))
    if opposite:

        @pl.when(zh < 2)
        def _():
            each(0, ny, lambda dy: hello(at_ka(dy, 2)))

    each(1, nzl, lambda d: hello(at_zl(d)))
    each(1, nx, lambda d: hello(at_row(d)))
    hello(partner)
    load_w.start()
    load_q.start()

    load_cond.wait()
    condt[...] = cond_v[...].T.reshape(condt.shape)
    load_ex.wait()
    half_cond = condt[:, co].reshape(nka * 16, nc)
    psend[...] = (
        lax.dot_general(half_cond, ex_v[zl], NT, preferred_element_type=F32)
        .astype(BF16)
        .reshape(psend.shape)
    )
    own_cond = jnp.concatenate([condt[i * nzh + zh].reshape(32, nc) for i in range(ny)], axis=0)
    for b in range(nzl):
        own = lax.dot_general(own_cond, ex_v[b], NT, preferred_element_type=F32)
        powns[:, b] = own.astype(BF16).reshape(ny, 2, 16, nv)
    pb[zh, y] = powns[y]
    load_val.wait()
    greeted = ny * len(beside) + nzl + nx - 2
    if opposite:
        greeted = greeted + ny * (zh // 2)
    pl.semaphore_wait(barrier, greeted)

    if opposite:

        @pl.when(zh >= 2)
        def _():
            def p_far(dy):
                to = ((y + dy) % ny) * nzh + zof(2)
                send(psend.at[to], pb.at[zh, y, zl, co], p1s.at[2], p1r.at[2], at_ka(dy, 2))

            each(0, ny, p_far)
            for u in range(2):
                part = vb.at[zh, y, r, u]
                send(part, part, vgs.at[u], vxr.at[u], at_ka(0, 2))

        @pl.when(zh < 2)
        def _():
            way = y // hy

            def p_far(dy):
                to_y = (y + dy) % ny
                send(
                    psend.at[to_y * nzh + zof(2)], prel.at[way, y % hy], p1s.at[2],
                    prr.at[way], {"ka": to_y * nzh + zof(1 + (nzh - 2) * way)},
                )

            each(0, ny, p_far)

    for dz in beside[1:]:
        part = vb.at[zh, y, r]
        send(part, part, v1s.at[dz], v1r.at[(nzh - dz) % nzh], at_ka(0, dz))

    for dz in reversed(beside[1:]):

        def p1(dy, dz=dz):
            to = ((y + dy) % ny) * nzh + zof(dz)
            send(
                psend.at[to], pb.at[zh, y, zl, co], p1s.at[dz], p1r.at[(nzh - dz) % nzh],
                at_ka(dy, dz),
            )

        each(0, ny, p1)

    def p_own(dy):
        send(powns.at[(y + dy) % ny], pb.at[zh, y], p1s.at[0], p1r.at[0], at_ka(dy, 0))

    each(1, ny, p_own)

    def relay(u):
        zs, on = zof(nzh - 1 + 2 * u), zof(nzh + 1 - 2 * u)
        got(vb.at[zs, y, r], v1r.at[(nzh - 1 + 2 * u) % nzh])
        part = vb.at[zs, y, r, u]
        send(part, part, vfs.at[0], vxr.at[u], {"ka": y * nzh + on})
        got(prel.at[u], prr.at[u])
        send(
            prel.at[u], pb.at[zs, pl.ds(u * hy, hy), zl, co], pfs.at[0], p1r.at[2],
            {"ka": y * nzh + on},
        )

    def first(d, far=False, own=False, relayed=False):
        zs = zof(d)
        if far:
            got(vb.at[zs, y, r, 0], vxr.at[0])
            got(vb.at[zs, y, r, 1], vxr.at[1])
        elif not (own or relayed):
            got(vb.at[zs, y, r], v1r.at[d])

        def v2a(e):
            part = vb.at[zs, y, r, 0]
            send(part, part, vas.at[d], var.at[d], at_ka(e, 0))

        def v2b(e):
            part = vb.at[zs, y, r, 1]
            send(part, part, vbs.at[d], vbr.at[d], at_row(e))

        def v_all(e):
            part = vb.at[zs, y, r]
            ex, ey = e // ny, e % ny
            where = {"ka": ((y + ey) % ny) * nzh + zh, "row": (r + ex) % nx}
            send(part, part, vys.at[ex], vyr.at[ex], where)

        if far:
            each(1, nx * ny, v_all)
        else:
            each(1, ny, v2a)
            each(1, nx, v2b)
        if own:
            return
        got(pb.at[zs, :, zl, co], p1r.at[d])

        def p2(e):
            part = pb.at[zs, :, zl, co]
            send(part, part, p2s.at[d], p2r.at[d], at_zl(e))

        each(1, nzl, p2)

    def second_panels(d):
        zs = zof(d)
        if nzl > 1:
            got(pb.at[zs, :, 0 : nzl - 1, co], p2r.at[d])
        part = pb.at[zs, :, :, co]
        send(part, part, pcs.at[d], pcr.at[d], partner)

    def second(d, own=False):
        zs = zof(d)
        if ny > 1:
            got(vb.at[zs, 0 : ny - 1, r, 0], var.at[d])

        def v3a(e):
            part = vb.at[zs, :, r, 0]
            send(part, part, vcs.at[d], vcr.at[d], at_row(e))

        each(1, nx, v3a)
        if nx > 1:
            got(vb.at[zs, y, 0 : nx - 1, 1], vbr.at[d])

        def v3b(e):
            part = vb.at[zs, y, :, 1]
            send(part, part, vds.at[d], vdr.at[d], at_ka(e, 0))

        each(1, ny, v3b)
        if not own:
            second_panels(d)

    def third(d, far=False, own=False):
        zs = zof(d)
        if not own:
            got(pb.at[zs, :, :, co], pcr.at[d])
        elif ny > 1:
            got(pb.at[zs, 0 : ny - 1], p1r.at[0])
        if far:
            if ny > 1:
                got(vb.at[zs, 0 : ny - 1, r], vyr.at[0])
            each(1, nx, lambda e: got(vb.at[zs, :, r], vyr.at[e]))
        else:
            if nx > 1:
                got(vb.at[zs, :, 0 : nx - 1, 0], vcr.at[d])
            if ny > 1:
                got(vb.at[zs, 0 : ny - 1, :, 1], vdr.at[d])

        for i in range(ny):
            panel = pb[zs, i].reshape(rows, nv)
            val = vb[zs, i].reshape(nv, nnu)
            pairs[zs, i] = jnp.dot(panel, val, preferred_element_type=F32).reshape(nzl, 32, nnu)

    lanes = nnu // 128

    def weigh(e, sources, start=False):
        zk = zof(e)

        def tile(t, carry):
            s = pl.ds(pl.multiple_of(t * 8, 8), 8)
            blocks = [pl.ds(l * 128, 128) for l in range(lanes)]
            place = [(i, b, l) for i in range(ny) for b in range(nzl) for l in range(lanes)]
            sums = {
                (i, b, l): None if start else direct[zk, i, b, s, blocks[l]] for i, b, l in place
            }
            for d in sources:
                z2 = zof(d)
                for y2 in range(ny):
                    p = [[pairs[z2, y2, b, s, m] for m in blocks] for b in range(nzl)]
                    for i in range(ny):
                        q = q_ref[y2 * nzh + z2, i * nzh + zk]
                        for l in range(lanes):
                            w = wf[q, s, blocks[l]]
                            for b in range(nzl):
                                term = w * p[b][l]
                                old = sums[i, b, l]
                                sums[i, b, l] = term if old is None else old + term
            for i, b, l in place:
                direct[zk, i, b, s, blocks[l]] = sums[i, b, l]
            return carry

        lax.fori_loop(0, 4, tile, 0)

    def weigh_all(sources, lo, hi, start=False):
        def step(e, carry):
            weigh(e, sources, start)
            return carry

        lax.fori_loop(lo, hi, step, 0)

    first(0, own=True)
    load_w.wait()
    load_q.wait()
    wf[...] = w_v[...].astype(F32)
    for k in range(nka):
        for b in range(nzl):
            ct4[k % nzh, k // nzh, b] = condt[k].reshape(32, nc)

    if opposite:
        u0 = ((zh + 1) // 2 + 1) % 2
        u1 = 1 - u0
        d0, d1 = (nzh - 1 + 2 * u0) % nzh, (nzh - 1 + 2 * u1) % nzh
        second(0, own=True)
        relay(u0)
        first(d0, relayed=True)
        first(d1)
        third(0, own=True)
        weigh_all((0,), 0, nzh, True)
        second(d0)
        first(2, far=True)
        second(d1)
        third(d0)
        before = nzh * (1 - zh // 2)
        weigh_all((d0,), 0, before)
        second_panels(2)
        weigh_all((d0,), before, nzh)
        third(d1)
        third(2, far=True)
        late = (d1, 2)
    else:
        for d in near[1:]:
            first(d)
        for d in near:
            second(d, own=d == 0)
        third(0, own=True)
        weigh_all((0,), 0, nzh, True)
        for d in near[1:]:
            third(d)
        late = tuple(near[1:])

    def halves(e):
        zk = zof(e)

        for i in range(ny):
            d = direct[zk, i].reshape(rows, nnu).astype(BF16)
            val = vb[zk, i].reshape(nv, nnu)
            h = lax.dot_general(val, d, NT, preferred_element_type=F32)
            hs[zk, i] = h.astype(BF16).reshape(nzl, 2, 16, rows)
        send(hs.at[zk, :, :, 1 - co], c1.at[zk], h1s.at[e], h1r.at[e], partner)

    def over_zl(e):
        zk = zof(e)
        got(c1.at[zk], h1r.at[e])

        def add_core(i, carry):
            tsum[zk, :, i] = (hs[zk, i, :, co].astype(F32) + c1[zk, i].astype(F32)).astype(BF16)
            return carry

        lax.fori_loop(0, ny, add_core, 0)

        def h2(d):
            send(
                tsum.at[zk, (zl + d) % nzl], zr.at[zk, d], h2s.at[e], h2r.at[e], at_zl(d)
            )

        each(1, nzl, h2)

    def over_ka(e):
        zk = zof(e)
        if nzl > 1:
            got(zr.at[zk, 0 : nzl - 1], h2r.at[e])

        def add_zl(i, carry):
            total = tsum[zk, zl, i].astype(F32)
            for d in range(1, nzl):
                total = total + zr[zk, d, i].astype(F32)
            us[zk, i] = total.astype(BF16)
            return carry

        lax.fori_loop(0, ny, add_zl, 0)

        def h3(dy):
            send(
                us.at[zk, (y + dy) % ny], fr.at[zh, y], h3s.at[e], h3r.at[(nzh - e) % nzh],
                at_ka(dy, e),
            )

        each(1 if e == 0 else 0, ny, h3)
        if e == 0:
            fr[zh, y] = us[zh, y]

    far = near[::-1]
    for i, e in enumerate(far):
        if late:
            weigh(e, late)
        halves(e)
        if i:
            over_zl(far[i - 1])
    over_zl(far[-1])
    for e in far:
        over_ka(e)

    lane_b = lax.broadcasted_iota(jnp.int32, (16, rows), 1) // 32
    total = jnp.zeros((nzl * 16, nc), F32)
    for d in near[1:] + near[:1]:
        have = ny if d else ny - 1
        zs = zof(d)
        if have:
            got(fr.at[zs, 0:have], h3r.at[d])
        for i in range(ny):
            f = fr[zs, i].astype(F32)
            lhs = jnp.concatenate(
                [jnp.where(lane_b == b, f, 0.0) for b in range(nzl)], axis=0
            ).astype(BF16)
            total = total + jnp.dot(
                lhs, ct4[zs, i].reshape(rows, nc), preferred_element_type=F32
            )
    xs[r] = total.astype(BF16)

    def h5(d):
        send(xs.at[r], xs.at[r], h5s.at[0], h5r.at[0], at_row(d))

    each(1, nx, h5)

    for d in range(nzh):
        if d in beside[1:]:
            got(vb.at[zh, y, r], v1s.at[d])
        if d:
            got(pb.at[zh, :, zl, co], p1s.at[d])
            got(pb.at[zh, :, :, co], pcs.at[d])
            if nzl > 1:
                got(pb.at[zh, :, 0 : nzl - 1, co], p2s.at[d])
        elif ny > 1:
            got(pb.at[zh, 0 : ny - 1], p1s.at[0])
        if d == 2 and opposite:
            if ny > 1:
                got(vb.at[zh, 0 : ny - 1, r], vys.at[0])
            each(1, nx, lambda e: got(vb.at[zh, :, r], vys.at[e]))
        else:
            if ny > 1:
                got(vb.at[zh, 0 : ny - 1, r, 0], vas.at[d])
                got(vb.at[zh, 0 : ny - 1, :, 1], vds.at[d])
            if nx > 1:
                got(vb.at[zh, y, 0 : nx - 1, 1], vbs.at[d])
                got(vb.at[zh, :, 0 : nx - 1, 0], vcs.at[d])
        got(c1.at[zh], h1s.at[d])
        if nzl > 1:
            got(zr.at[zh, 0 : nzl - 1], h2s.at[d])
        if d or ny > 1:
            got(fr.at[zh, 0 : ny if d else ny - 1], h3s.at[d])
    if opposite:
        got(vb.at[zh, y, r, 0], vfs.at[0])
        got(prel.at[0], pfs.at[0])

        @pl.when(zh >= 2)
        def _():
            for u in range(2):
                got(vb.at[zh, y, r, u], vgs.at[u])

    if nx > 1:
        got(xs.at[0 : nx - 1], h5r.at[0])
    result = xs[0].astype(F32)
    for i in range(1, nx):
        result = result + xs[i].astype(F32)
    out_ref[...] = (result * factor).reshape(out_ref.shape)

    if nx > 1:
        got(xs.at[0 : nx - 1], h5s.at[0])


def local(sizes, factor, exciton, orb_cond, orb_val, screened, q_table):
    ny, nzh, nx, nzl = sizes
    nka = ny * nzh
    nc = exciton.shape[-1]
    nv = nzl * 32
    rows = nzl * 32
    mu = nka * 32
    nnu = orb_val.shape[-1]
    any_space = pl.BlockSpec(memory_space=pl.ANY)
    dma = lambda *n: pltpu.SemaphoreType.DMA(n)
    vm = pltpu.VMEM
    out = pl.pallas_call(
        functools.partial(kernel, sizes, factor),
        name="isdf_direct",
        out_shape=jax.ShapeDtypeStruct((nzl, 16, nc), F32),
        in_specs=[any_space] * 5,
        out_specs=pl.BlockSpec(memory_space=pltpu.VMEM),
        scratch_shapes=[
            pltpu.SMEM((nka, nka), jnp.int32),
            vm((nzl, nv, nc), BF16),
            vm((nc, mu), BF16),
            vm((nka, 2, 16, nc), BF16),
            vm((nzh, ny, nzl, 32, nc), BF16),
            vm((nka, 32, nnu), BF16),
            vm((nka, 32, nnu), F32),
            vm((nka, 16, nv), BF16),
            vm((ny, nzl, 2, 16, nv), BF16),
            vm((2, max(1, ny // 2), 16, nv), BF16),
            vm((nzh, ny, nzl, 2, 16, nv), BF16),
            vm((nzh, ny, nx, 2, 16, nnu), BF16),
            vm((nzh, ny, nzl, 32, nnu), F32),
            vm((nzh, ny, nzl, 32, nnu), F32),
            vm((nzh, ny, nzl, 2, 16, rows), BF16),
            vm((nzh, ny, nzl, 16, rows), BF16),
            vm((nzh, nzl, ny, 16, rows), BF16),
            vm((nzh, nzl, ny, 16, rows), BF16),
            vm((nzh, ny, 16, rows), BF16),
            vm((nzh, ny, 16, rows), BF16),
            vm((nx, nzl * 16, nc), BF16),
            dma(5),
            dma(nzh), dma(nzh), dma(2), dma(1),
            dma(nzh), dma(nzh), dma(nzh), dma(nzh),
            dma(nzh), dma(nzh), dma(2), dma(1), dma(2), dma(nx), dma(nx),
            dma(nzh), dma(nzh), dma(nzh), dma(nzh),
            dma(nzh), dma(nzh), dma(nzh), dma(nzh),
            dma(nzh), dma(nzh), dma(nzh), dma(nzh),
            dma(nzh), dma(nzh), dma(1), dma(1),
        ],
        compiler_params=pltpu.CompilerParams(
            collective_id=0, has_side_effects=True, vmem_limit_bytes=56 * 1024 * 1024
        ),
    )(
        q_table,
        exciton[0],
        orb_cond[0],
        orb_val.reshape(nx, 2, 16, nnu),
        screened.reshape(nka, nka, 32, nnu),
    )
    return out[None]


def build(mesh, nzh, factor):
    shape = mesh.shape
    sizes = (shape["ka"] // nzh, nzh, shape["row"], shape["col"] // 2)
    placed = (
        P("ka", None, None, None),
        P("ka", None, "row"),
        P("ka", None, "col"),
        P(None, "row", "col"),
        P(),
    )
    return jax.shard_map(
        functools.partial(local, sizes, factor),
        mesh=mesh, in_specs=placed, out_specs=P("ka", None, "col", None), check_vma=False,
    )


def solution(mesh):
    return build(mesh, NZH, math.sqrt(128 * 128) / 2048)
```

```python
import functools
import math

import jax
import jax.numpy as jnp
from jax import lax
from jax.experimental import pallas as pl
from jax.experimental.pallas import tpu as pltpu
from jax.sharding import PartitionSpec as P

NZH = 4
MESH = pl.DeviceIdType.MESH
BF16 = jnp.bfloat16
F32 = jnp.float32
NT = (((1,), (1,)), ((), ()))


def kernel(
    sizes, factor, q_hbm, ex_hbm, cond_hbm, val_hbm, w_hbm, out_ref,
    q_ref, ex_v, cond_v, condt, ct4, w_v, wf, psend, powns, prel, pb, vb, pairs, direct, hs, c1, tsum, zr, us, fr, xs,
    ld, p1s, p1r, prr, pfs, p2s, p2r, pcs, pcr, v1s, v1r, vxr, vfs, vgs, vys, vyr, vas, var, vbs, vbr, vcs, vcr, vds, vdr,
    h1s, h1r, h2s, h2r, h3s, h3r, h5s, h5r,
):
    ny, nzh, nx, nzl = sizes
    nka = ny * nzh
    rows, nv, nnu, nc = nzl * 32, nzl * 32, vb.shape[-1], condt.shape[-1]
    a, r, c = lax.axis_index("ka"), lax.axis_index("row"), lax.axis_index("col")
    y, zh = a // nzh, a % nzh
    zl, co = c // 2, c % 2
    partner = {"col": zl * 2 + 1 - co}
    near = sorted(range(nzh), key=lambda d: min(d, nzh - d))
    beside = [d for d in near if min(d, nzh - d) < 2]
    opposite = nzh > 2
    hy = ny // 2

    def at_ka(dy, dz):
        return {"ka": ((y + dy) % ny) * nzh + (zh + dz) % nzh}

    def at_zl(d):
        return {"col": ((zl + d) % nzl) * 2 + co}

    def at_row(d):
        return {"row": (r + d) % nx}

    def zof(d):
        return (zh + d) % nzh

    def send(src, dst, ss, rs, where):
        pltpu.make_async_remote_copy(
            src_ref=src, dst_ref=dst, send_sem=ss, recv_sem=rs, device_id=where, device_id_type=MESH
        ).start()

    def got(ref, rs):
        pltpu.make_async_copy(ref, ref, rs).wait()

    def each(lo, hi, body):
        def step(d, carry):
            body(d)
            return carry

        if hi > lo:
            lax.fori_loop(lo, hi, step, 0)

    load_ex = pltpu.make_async_copy(ex_hbm, ex_v, ld.at[0])
    load_cond = pltpu.make_async_copy(cond_hbm, cond_v, ld.at[1])
    load_val = pltpu.make_async_copy(val_hbm.at[r], vb.at[zh, y, r], ld.at[2])
    load_w = pltpu.make_async_copy(w_hbm.at[:, a], w_v, ld.at[3])
    load_q = pltpu.make_async_copy(q_hbm, q_ref, ld.at[4])
    load_cond.start()
    load_ex.start()
    load_val.start()

    barrier = pltpu.get_barrier_semaphore()

    def hello(where):
        pl.semaphore_signal(barrier, inc=1, device_id=where, device_id_type=MESH)

    for dz in reversed(beside):
        each(1 if dz == 0 else 0, ny, lambda dy: hello(at_ka(dy, dz)))
    if opposite:

        @pl.when(zh < 2)
        def _():
            each(0, ny, lambda dy: hello(at_ka(dy, 2)))

    each(1, nzl, lambda d: hello(at_zl(d)))
    each(1, nx, lambda d: hello(at_row(d)))
    hello(partner)
    load_w.start()
    load_q.start()

    load_cond.wait()
    condt[...] = cond_v[...].T.reshape(condt.shape)
    load_ex.wait()
    half_cond = condt[:, co].reshape(nka * 16, nc)
    psend[...] = (
        lax.dot_general(half_cond, ex_v[zl], NT, preferred_element_type=F32)
        .astype(BF16)
        .reshape(psend.shape)
    )
    own_cond = jnp.concatenate([condt[i * nzh + zh].reshape(32, nc) for i in range(ny)], axis=0)
    for b in range(nzl):
        own = lax.dot_general(own_cond, ex_v[b], NT, preferred_element_type=F32)
        powns[:, b] = own.astype(BF16).reshape(ny, 2, 16, nv)
    pb[zh, y] = powns[y]
    load_val.wait()
    greeted = ny * len(beside) + nzl + nx - 2
    if opposite:
        greeted = greeted + ny * (zh // 2)
    pl.semaphore_wait(barrier, greeted)

    if opposite:

        @pl.when(zh >= 2)
        def _():
            def p_far(dy):
                to = ((y + dy) % ny) * nzh + zof(2)
                send(psend.at[to], pb.at[zh, y, zl, co], p1s.at[0], p1r.at[2], at_ka(dy, 2))

            each(0, ny, p_far)
            for u in range(2):
                part = vb.at[zh, y, r, u]
                send(part, part, vgs.at[0], vxr.at[u], at_ka(0, 2))

        @pl.when(zh < 2)
        def _():
            way = y // hy

            def p_far(dy):
                to_y = (y + dy) % ny
                send(
                    psend.at[to_y * nzh + zof(2)], prel.at[way, y % hy], p1s.at[0],
                    prr.at[way], {"ka": to_y * nzh + zof(1 + (nzh - 2) * way)},
                )

            each(0, ny, p_far)

    for dz in beside[1:]:
        part = vb.at[zh, y, r]
        send(part, part, v1s.at[0], v1r.at[(nzh - dz) % nzh], at_ka(0, dz))

    for dz in reversed(beside[1:]):

        def p1(dy, dz=dz):
            to = ((y + dy) % ny) * nzh + zof(dz)
            send(
                psend.at[to], pb.at[zh, y, zl, co], p1s.at[0], p1r.at[(nzh - dz) % nzh],
                at_ka(dy, dz),
            )

        each(0, ny, p1)

    def p_own(dy):
        send(powns.at[(y + dy) % ny], pb.at[zh, y], p1s.at[1], p1r.at[0], at_ka(dy, 0))

    each(1, ny, p_own)

    def relay(u):
        zs, on = zof(nzh - 1 + 2 * u), zof(nzh + 1 - 2 * u)
        got(vb.at[zs, y, r], v1r.at[(nzh - 1 + 2 * u) % nzh])
        part = vb.at[zs, y, r, u]
        send(part, part, vfs.at[0], vxr.at[u], {"ka": y * nzh + on})
        got(prel.at[u], prr.at[u])
        send(
            prel.at[u], pb.at[zs, pl.ds(u * hy, hy), zl, co], pfs.at[0], p1r.at[2],
            {"ka": y * nzh + on},
        )

    def first(d, far=False, own=False, relayed=False):
        zs = zof(d)
        if far:
            got(vb.at[zs, y, r, 0], vxr.at[0])
            got(vb.at[zs, y, r, 1], vxr.at[1])
        elif not (own or relayed):
            got(vb.at[zs, y, r], v1r.at[d])

        def v2a(e):
            part = vb.at[zs, y, r, 0]
            send(part, part, vas.at[0], var.at[d], at_ka(e, 0))

        def v2b(e):
            part = vb.at[zs, y, r, 1]
            send(part, part, vbs.at[0], vbr.at[d], at_row(e))

        def v_all(e, other):
            part = vb.at[zs, y, r]
            ex, ey = e // ny, e % ny
            where = {"ka": ((y + ey) % ny) * nzh + zh, "row": (r + ex) % nx}
            send(part, part, vys.at[other], vyr.at[other], where)

        if far:
            each(1, ny, lambda e: v_all(e, 0))
            each(ny, nx * ny, lambda e: v_all(e, 1))
        else:
            each(1, ny, v2a)
            each(1, nx, v2b)
        if own:
            return
        got(pb.at[zs, :, zl, co], p1r.at[d])

        def p2(e):
            part = pb.at[zs, :, zl, co]
            send(part, part, p2s.at[0], p2r.at[d], at_zl(e))

        each(1, nzl, p2)

    def second_panels(d):
        zs = zof(d)
        if nzl > 1:
            got(pb.at[zs, :, 0 : nzl - 1, co], p2r.at[d])
        part = pb.at[zs, :, :, co]
        send(part, part, pcs.at[0], pcr.at[d], partner)

    def second(d, own=False):
        zs = zof(d)
        if ny > 1:
            got(vb.at[zs, 0 : ny - 1, r, 0], var.at[d])

        def v3a(e):
            part = vb.at[zs, :, r, 0]
            send(part, part, vcs.at[0], vcr.at[d], at_row(e))

        each(1, nx, v3a)
        if nx > 1:
            got(vb.at[zs, y, 0 : nx - 1, 1], vbr.at[d])

        def v3b(e):
            part = vb.at[zs, y, :, 1]
            send(part, part, vds.at[0], vdr.at[d], at_ka(e, 0))

        each(1, ny, v3b)
        if not own:
            second_panels(d)

    def third(d, far=False, own=False):
        zs = zof(d)
        if not own:
            got(pb.at[zs, :, :, co], pcr.at[d])
        elif ny > 1:
            got(pb.at[zs, 0 : ny - 1], p1r.at[0])
        if far:
            if ny > 1:
                got(vb.at[zs, 0 : ny - 1, r], vyr.at[0])
            if nx > 1:
                got(vb.at[0 : nx - 1, :, r], vyr.at[1])
        else:
            if nx > 1:
                got(vb.at[zs, :, 0 : nx - 1, 0], vcr.at[d])
            if ny > 1:
                got(vb.at[zs, 0 : ny - 1, :, 1], vdr.at[d])

        for i in range(ny):
            panel = pb[zs, i].reshape(rows, nv)
            val = vb[zs, i].reshape(nv, nnu)
            pairs[zs, i] = jnp.dot(panel, val, preferred_element_type=F32).reshape(nzl, 32, nnu)

    lanes = nnu // 128

    def weigh(e, sources, start=False):
        zk = zof(e)

        def tile(t, carry):
            s = pl.ds(pl.multiple_of(t * 8, 8), 8)
            blocks = [pl.ds(l * 128, 128) for l in range(lanes)]
            place = [(i, b, l) for i in range(ny) for b in range(nzl) for l in range(lanes)]
            sums = {
                (i, b, l): None if start else direct[zk, i, b, s, blocks[l]] for i, b, l in place
            }
            for d in sources:
                z2 = zof(d)
                for y2 in range(ny):
                    p = [[pairs[z2, y2, b, s, m] for m in blocks] for b in range(nzl)]
                    for i in range(ny):
                        q = q_ref[y2 * nzh + z2, i * nzh + zk]
                        for l in range(lanes):
                            w = wf[q, s, blocks[l]]
                            for b in range(nzl):
                                term = w * p[b][l]
                                old = sums[i, b, l]
                                sums[i, b, l] = term if old is None else old + term
            for i, b, l in place:
                direct[zk, i, b, s, blocks[l]] = sums[i, b, l]
            return carry

        lax.fori_loop(0, 4, tile, 0)

    def weigh_all(sources, lo, hi, start=False):
        def step(e, carry):
            weigh(e, sources, start)
            return carry

        lax.fori_loop(lo, hi, step, 0)

    first(0, own=True)
    load_w.wait()
    load_q.wait()
    wf[...] = w_v[...].astype(F32)
    for k in range(nka):
        for b in range(nzl):
            ct4[k % nzh, k // nzh, b] = condt[k].reshape(32, nc)

    if opposite:
        u0 = ((zh + 1) // 2 + 1) % 2
        u1 = 1 - u0
        d0, d1 = (nzh - 1 + 2 * u0) % nzh, (nzh - 1 + 2 * u1) % nzh
        second(0, own=True)
        relay(u0)
        first(d0, relayed=True)
        first(d1)
        third(0, own=True)
        weigh_all((0,), 0, nzh, True)
        second(d0)
        first(2, far=True)
        second(d1)
        third(d0)
        before = nzh * (1 - zh // 2)
        weigh_all((d0,), 0, before)
        second_panels(2)
        weigh_all((d0,), before, nzh)
        third(d1)
        third(2, far=True)
        late = (d1, 2)
    else:
        for d in near[1:]:
            first(d)
        for d in near:
            second(d, own=d == 0)
        third(0, own=True)
        weigh_all((0,), 0, nzh, True)
        for d in near[1:]:
            third(d)
        late = tuple(near[1:])

    def halves(e):
        zk = zof(e)

        for i in range(ny):
            d = direct[zk, i].reshape(rows, nnu).astype(BF16)
            val = vb[zk, i].reshape(nv, nnu)
            h = lax.dot_general(val, d, NT, preferred_element_type=F32)
            hs[zk, i] = h.astype(BF16).reshape(nzl, 2, 16, rows)
        send(hs.at[zk, :, :, 1 - co], c1.at[zk], h1s.at[0], h1r.at[e], partner)

    def over_zl(e):
        zk = zof(e)
        got(c1.at[zk], h1r.at[e])

        def add_core(i, carry):
            tsum[zk, :, i] = (hs[zk, i, :, co].astype(F32) + c1[zk, i].astype(F32)).astype(BF16)
            return carry

        lax.fori_loop(0, ny, add_core, 0)

        def h2(d):
            send(
                tsum.at[zk, (zl + d) % nzl], zr.at[zk, d], h2s.at[0], h2r.at[e], at_zl(d)
            )

        each(1, nzl, h2)

    def over_ka(e):
        zk = zof(e)
        if nzl > 1:
            got(zr.at[zk, 0 : nzl - 1], h2r.at[e])

        def add_zl(i, carry):
            total = tsum[zk, zl, i].astype(F32)
            for d in range(1, nzl):
                total = total + zr[zk, d, i].astype(F32)
            us[zk, i] = total.astype(BF16)
            return carry

        lax.fori_loop(0, ny, add_zl, 0)

        def h3(dy):
            send(
                us.at[zk, (y + dy) % ny], fr.at[zh, y], h3s.at[0 if e else 1], h3r.at[(nzh - e) % nzh],
                at_ka(dy, e),
            )

        each(1 if e == 0 else 0, ny, h3)
        if e == 0:
            fr[zh, y] = us[zh, y]

    far = near[::-1]
    for i, e in enumerate(far):
        if late:
            weigh(e, late)
        halves(e)
        if i:
            over_zl(far[i - 1])
    over_zl(far[-1])
    for e in far:
        over_ka(e)

    lane_b = lax.broadcasted_iota(jnp.int32, (16, rows), 1) // 32
    total = jnp.zeros((nzl * 16, nc), F32)
    for d in near[1:] + near[:1]:
        have = ny if d else ny - 1
        zs = zof(d)
        if have:
            got(fr.at[zs, 0:have], h3r.at[d])
        for i in range(ny):
            f = fr[zs, i].astype(F32)
            lhs = jnp.concatenate(
                [jnp.where(lane_b == b, f, 0.0) for b in range(nzl)], axis=0
            ).astype(BF16)
            total = total + jnp.dot(
                lhs, ct4[zs, i].reshape(rows, nc), preferred_element_type=F32
            )
    xs[r] = total.astype(BF16)

    def h5(d):
        send(xs.at[r], xs.at[r], h5s.at[0], h5r.at[0], at_row(d))

    each(1, nx, h5)

    legs = nzh - 1 if opposite else nzh
    if nzh > 1:
        got(vb.at[0 : len(beside) - 1, y, r], v1s.at[0])
        got(pb.at[0 : nzh - 1, :, zl, co], p1s.at[0])
        got(pb.at[0 : nzh - 1, :, :, co], pcs.at[0])
        got(fr.at[0 : nzh - 1], h3s.at[0])
        if nzl > 1:
            got(pb.at[0 : nzh - 1, :, 0 : nzl - 1, co], p2s.at[0])
    if ny > 1:
        got(pb.at[zh, 0 : ny - 1], p1s.at[1])
        got(fr.at[zh, 0 : ny - 1], h3s.at[1])
        got(vb.at[0:legs, 0 : ny - 1, r, 0], vas.at[0])
        got(vb.at[0:legs, 0 : ny - 1, :, 1], vds.at[0])
    if nx > 1:
        got(vb.at[0:legs, y, 0 : nx - 1, 1], vbs.at[0])
        got(vb.at[0:legs, :, 0 : nx - 1, 0], vcs.at[0])
    got(c1, h1s.at[0])
    if nzl > 1:
        got(zr.at[:, 0 : nzl - 1], h2s.at[0])
    if opposite:
        if ny > 1:
            got(vb.at[zh, 0 : ny - 1, r], vys.at[0])
        if nx > 1:
            got(vb.at[0 : nx - 1, :, r], vys.at[1])
        got(vb.at[zh, y, r, 0], vfs.at[0])
        got(prel.at[0], pfs.at[0])

        @pl.when(zh >= 2)
        def _():
            got(vb.at[zh, y, r], vgs.at[0])

    if nx > 1:
        got(xs.at[0 : nx - 1], h5r.at[0])
    result = xs[0].astype(F32)
    for i in range(1, nx):
        result = result + xs[i].astype(F32)
    out_ref[...] = (result * factor).reshape(out_ref.shape)

    if nx > 1:
        got(xs.at[0 : nx - 1], h5s.at[0])


def local(sizes, factor, exciton, orb_cond, orb_val, screened, q_table):
    ny, nzh, nx, nzl = sizes
    nka = ny * nzh
    nc = exciton.shape[-1]
    nv = nzl * 32
    rows = nzl * 32
    mu = nka * 32
    nnu = orb_val.shape[-1]
    any_space = pl.BlockSpec(memory_space=pl.ANY)
    dma = lambda *n: pltpu.SemaphoreType.DMA(n)
    vm = pltpu.VMEM
    out = pl.pallas_call(
        functools.partial(kernel, sizes, factor),
        name="isdf_direct",
        out_shape=jax.ShapeDtypeStruct((nzl, 16, nc), F32),
        in_specs=[any_space] * 5,
        out_specs=pl.BlockSpec(memory_space=pltpu.VMEM),
        scratch_shapes=[
            pltpu.SMEM((nka, nka), jnp.int32),
            vm((nzl, nv, nc), BF16),
            vm((nc, mu), BF16),
            vm((nka, 2, 16, nc), BF16),
            vm((nzh, ny, nzl, 32, nc), BF16),
            vm((nka, 32, nnu), BF16),
            vm((nka, 32, nnu), F32),
            vm((nka, 16, nv), BF16),
            vm((ny, nzl, 2, 16, nv), BF16),
            vm((2, max(1, ny // 2), 16, nv), BF16),
            vm((nzh, ny, nzl, 2, 16, nv), BF16),
            vm((nzh, ny, nx, 2, 16, nnu), BF16),
            vm((nzh, ny, nzl, 32, nnu), F32),
            vm((nzh, ny, nzl, 32, nnu), F32),
            vm((nzh, ny, nzl, 2, 16, rows), BF16),
            vm((nzh, ny, nzl, 16, rows), BF16),
            vm((nzh, nzl, ny, 16, rows), BF16),
            vm((nzh, nzl, ny, 16, rows), BF16),
            vm((nzh, ny, 16, rows), BF16),
            vm((nzh, ny, 16, rows), BF16),
            vm((nx, nzl * 16, nc), BF16),
            dma(5),
            dma(2), dma(nzh), dma(2), dma(1),
            dma(1), dma(nzh), dma(1), dma(nzh),
            dma(1), dma(nzh), dma(2), dma(1), dma(1), dma(2), dma(2),
            dma(1), dma(nzh), dma(1), dma(nzh),
            dma(1), dma(nzh), dma(1), dma(nzh),
            dma(1), dma(nzh), dma(1), dma(nzh),
            dma(2), dma(nzh), dma(1), dma(1),
        ],
        compiler_params=pltpu.CompilerParams(
            collective_id=0, has_side_effects=True, vmem_limit_bytes=56 * 1024 * 1024
        ),
    )(
        q_table,
        exciton[0],
        orb_cond[0],
        orb_val.reshape(nx, 2, 16, nnu),
        screened.reshape(nka, nka, 32, nnu),
    )
    return out[None]


def build(mesh, nzh, factor):
    shape = mesh.shape
    sizes = (shape["ka"] // nzh, nzh, shape["row"], shape["col"] // 2)
    placed = (
        P("ka", None, None, None),
        P("ka", None, "row"),
        P("ka", None, "col"),
        P(None, "row", "col"),
        P(),
    )
    return jax.shard_map(
        functools.partial(local, sizes, factor),
        mesh=mesh, in_specs=placed, out_specs=P("ka", None, "col", None), check_vma=False,
    )


def solution(mesh):
    return build(mesh, NZH, math.sqrt(128 * 128) / 2048)
```

```python
import functools
import math

import jax
import jax.numpy as jnp
from jax import lax
from jax.experimental import pallas as pl
from jax.experimental.pallas import tpu as pltpu
from jax.sharding import PartitionSpec as P

NZH = 4
MESH = pl.DeviceIdType.MESH
BF16 = jnp.bfloat16
F32 = jnp.float32
NT = (((1,), (1,)), ((), ()))


def kernel(
    sizes, factor, q_hbm, ex_hbm, cond_hbm, val_hbm, w_hbm, out_ref,
    q_ref, ex_v, cond_v, condt, ct4, w_v, wf, psend, powns, prel, pb, vb, pairs, direct, hs, c1, tsum, zr, us, fr, xs,
    ld, p1s, p1r, prr, pfs, p2s, p2r, pcs, pcr, v1s, v1r, vxr, vfs, vgs, vys, vyr, vas, var, vbs, vbr, vcs, vcr, vds, vdr,
    h1s, h1r, h2s, h2r, h3s, h3r, h5s, h5r,
):
    ny, nzh, nx, nzl = sizes
    nka = ny * nzh
    rows, nv, nnu, nc = nzl * 32, nzl * 32, vb.shape[-1], condt.shape[-1]
    a, r, c = lax.axis_index("ka"), lax.axis_index("row"), lax.axis_index("col")
    y, zh = a // nzh, a % nzh
    zl, co = c // 2, c % 2
    partner = {"col": zl * 2 + 1 - co}
    near = sorted(range(nzh), key=lambda d: min(d, nzh - d))
    beside = [d for d in near if min(d, nzh - d) < 2]
    opposite = nzh > 2
    hy = ny // 2

    def at_ka(dy, dz):
        return {"ka": ((y + dy) % ny) * nzh + (zh + dz) % nzh}

    def at_zl(d):
        return {"col": ((zl + d) % nzl) * 2 + co}

    def at_row(d):
        return {"row": (r + d) % nx}

    def leg_of(d):
        return d - d // 2 if opposite else d

    def zof(d):
        return (zh + d) % nzh

    def send(src, dst, ss, rs, where):
        pltpu.make_async_remote_copy(
            src_ref=src, dst_ref=dst, send_sem=ss, recv_sem=rs, device_id=where, device_id_type=MESH
        ).start()

    def got(ref, rs):
        pltpu.make_async_copy(ref, ref, rs).wait()

    def each(lo, hi, body):
        def step(d, carry):
            body(d)
            return carry

        if hi > lo:
            lax.fori_loop(lo, hi, step, 0)

    load_ex = pltpu.make_async_copy(ex_hbm, ex_v, ld.at[0])
    load_cond = pltpu.make_async_copy(cond_hbm, cond_v, ld.at[1])
    load_val = pltpu.make_async_copy(val_hbm.at[r], vb.at[zh, y, r], ld.at[2])
    load_w = pltpu.make_async_copy(w_hbm.at[:, a], w_v, ld.at[3])
    load_q = pltpu.make_async_copy(q_hbm, q_ref, ld.at[4])
    load_cond.start()
    load_ex.start()
    load_val.start()

    barrier = pltpu.get_barrier_semaphore()

    def hello(where):
        pl.semaphore_signal(barrier, inc=1, device_id=where, device_id_type=MESH)

    for dz in reversed(beside):
        each(1 if dz == 0 else 0, ny, lambda dy: hello(at_ka(dy, dz)))
    if opposite:

        @pl.when(zh < 2)
        def _():
            each(0, ny, lambda dy: hello(at_ka(dy, 2)))

    each(1, nzl, lambda d: hello(at_zl(d)))
    each(1, nx, lambda d: hello(at_row(d)))
    hello(partner)
    load_w.start()
    load_q.start()

    load_cond.wait()
    condt[...] = cond_v[...].T.reshape(condt.shape)
    load_ex.wait()
    half_cond = condt[:, co].reshape(nka * 16, nc)
    psend[...] = (
        lax.dot_general(half_cond, ex_v[zl], NT, preferred_element_type=F32)
        .astype(BF16)
        .reshape(psend.shape)
    )
    own_cond = jnp.concatenate([condt[i * nzh + zh].reshape(32, nc) for i in range(ny)], axis=0)
    for b in range(nzl):
        own = lax.dot_general(own_cond, ex_v[b], NT, preferred_element_type=F32)
        powns[:, b] = own.astype(BF16).reshape(ny, 2, 16, nv)
    pb[zh, y] = powns[y]
    load_val.wait()
    greeted = ny * len(beside) + nzl + nx - 2
    if opposite:
        greeted = greeted + ny * (zh // 2)
    pl.semaphore_wait(barrier, greeted)

    if opposite:

        @pl.when(zh >= 2)
        def _():
            def p_far(dy):
                to = ((y + dy) % ny) * nzh + zof(2)
                send(psend.at[to], pb.at[zh, y, zl, co], p1s.at[0], p1r.at[2], at_ka(dy, 2))

            each(0, ny, p_far)
            for u in range(2):
                part = vb.at[zh, y, r, u]
                send(part, part, vgs.at[0], vxr.at[u], at_ka(0, 2))

        @pl.when(zh < 2)
        def _():
            way = y // hy

            def p_far(dy):
                to_y = (y + dy) % ny
                send(
                    psend.at[to_y * nzh + zof(2)], prel.at[way, y % hy], p1s.at[0],
                    prr.at[way], {"ka": to_y * nzh + zof(1 + (nzh - 2) * way)},
                )

            each(0, ny, p_far)

    for dz in beside[1:]:
        part = vb.at[zh, y, r]
        send(part, part, v1s.at[0], v1r.at[(nzh - dz) % nzh // 2], at_ka(0, dz))

    for dz in reversed(beside[1:]):

        def p1(dy, dz=dz):
            to = ((y + dy) % ny) * nzh + zof(dz)
            send(
                psend.at[to], pb.at[zh, y, zl, co], p1s.at[0], p1r.at[(nzh - dz) % nzh],
                at_ka(dy, dz),
            )

        each(0, ny, p1)

    def p_own(dy):
        send(powns.at[(y + dy) % ny], pb.at[zh, y], p1s.at[1], p1r.at[0], at_ka(dy, 0))

    each(1, ny, p_own)

    def relay(u):
        zs, on = zof(nzh - 1 + 2 * u), zof(nzh + 1 - 2 * u)
        got(vb.at[zs, y, r], v1r.at[(nzh - 1 + 2 * u) % nzh // 2])
        part = vb.at[zs, y, r, u]
        send(part, part, vfs.at[0], vxr.at[u], {"ka": y * nzh + on})
        got(prel.at[u], prr.at[u])
        send(
            prel.at[u], pb.at[zs, pl.ds(u * hy, hy), zl, co], pfs.at[0], p1r.at[2],
            {"ka": y * nzh + on},
        )

    def first(d, far=False, own=False, relayed=False):
        zs = zof(d)
        if far:
            got(vb.at[zs, y, r, 0], vxr.at[0])
            got(vb.at[zs, y, r, 1], vxr.at[1])
        elif not (own or relayed):
            got(vb.at[zs, y, r], v1r.at[d // 2])

        def v2a(e):
            part = vb.at[zs, y, r, 0]
            send(part, part, vas.at[0], var.at[leg_of(d)], at_ka(e, 0))

        def v2b(e):
            part = vb.at[zs, y, r, 1]
            send(part, part, vbs.at[0], vbr.at[leg_of(d)], at_row(e))

        def v_all(e, other):
            part = vb.at[zs, y, r]
            ex, ey = e // ny, e % ny
            where = {"ka": ((y + ey) % ny) * nzh + zh, "row": (r + ex) % nx}
            send(part, part, vys.at[other], vyr.at[other], where)

        if far:
            each(1, ny, lambda e: v_all(e, 0))
            each(ny, nx * ny, lambda e: v_all(e, 1))
        else:
            each(1, ny, v2a)
            each(1, nx, v2b)
        if own:
            return
        got(pb.at[zs, :, zl, co], p1r.at[d])

        def p2(e):
            part = pb.at[zs, :, zl, co]
            send(part, part, p2s.at[0], p2r.at[d - 1], at_zl(e))

        each(1, nzl, p2)

    def second_panels(d):
        zs = zof(d)
        if nzl > 1:
            got(pb.at[zs, :, 0 : nzl - 1, co], p2r.at[d - 1])
        part = pb.at[zs, :, :, co]
        send(part, part, pcs.at[0], pcr.at[d - 1], partner)

    def second(d, own=False):
        zs = zof(d)
        if ny > 1:
            got(vb.at[zs, 0 : ny - 1, r, 0], var.at[leg_of(d)])

        def v3a(e):
            part = vb.at[zs, :, r, 0]
            send(part, part, vcs.at[0], vcr.at[leg_of(d)], at_row(e))

        each(1, nx, v3a)
        if nx > 1:
            got(vb.at[zs, y, 0 : nx - 1, 1], vbr.at[leg_of(d)])

        def v3b(e):
            part = vb.at[zs, y, :, 1]
            send(part, part, vds.at[0], vdr.at[leg_of(d)], at_ka(e, 0))

        each(1, ny, v3b)
        if not own:
            second_panels(d)

    def third(d, far=False, own=False):
        zs = zof(d)
        if not own:
            got(pb.at[zs, :, :, co], pcr.at[d - 1])
        elif ny > 1:
            got(pb.at[zs, 0 : ny - 1], p1r.at[0])
        if far:
            if ny > 1:
                got(vb.at[zs, 0 : ny - 1, r], vyr.at[0])
            if nx > 1:
                got(vb.at[0 : nx - 1, :, r], vyr.at[1])
        else:
            if nx > 1:
                got(vb.at[zs, :, 0 : nx - 1, 0], vcr.at[leg_of(d)])
            if ny > 1:
                got(vb.at[zs, 0 : ny - 1, :, 1], vdr.at[leg_of(d)])

        for i in range(ny):
            panel = pb[zs, i].reshape(rows, nv)
            val = vb[zs, i].reshape(nv, nnu)
            pairs[zs, i] = jnp.dot(panel, val, preferred_element_type=F32).reshape(nzl, 32, nnu)

    lanes = nnu // 128

    def weigh(e, sources, start=False):
        zk = zof(e)

        def tile(t, carry):
            s = pl.ds(pl.multiple_of(t * 8, 8), 8)
            blocks = [pl.ds(l * 128, 128) for l in range(lanes)]
            place = [(i, b, l) for i in range(ny) for b in range(nzl) for l in range(lanes)]
            sums = {
                (i, b, l): None if start else direct[zk, i, b, s, blocks[l]] for i, b, l in place
            }
            for d in sources:
                z2 = zof(d)
                for y2 in range(ny):
                    p = [[pairs[z2, y2, b, s, m] for m in blocks] for b in range(nzl)]
                    for i in range(ny):
                        q = q_ref[y2 * nzh + z2, i * nzh + zk]
                        for l in range(lanes):
                            w = wf[q, s, blocks[l]]
                            for b in range(nzl):
                                term = w * p[b][l]
                                old = sums[i, b, l]
                                sums[i, b, l] = term if old is None else old + term
            for i, b, l in place:
                direct[zk, i, b, s, blocks[l]] = sums[i, b, l]
            return carry

        lax.fori_loop(0, 4, tile, 0)

    def weigh_all(sources, lo, hi, start=False):
        def step(e, carry):
            weigh(e, sources, start)
            return carry

        lax.fori_loop(lo, hi, step, 0)

    first(0, own=True)
    load_w.wait()
    load_q.wait()
    wf[...] = w_v[...].astype(F32)
    for k in range(nka):
        for b in range(nzl):
            ct4[k % nzh, k // nzh, b] = condt[k].reshape(32, nc)

    if opposite:
        u0 = ((zh + 1) // 2 + 1) % 2
        u1 = 1 - u0
        d0, d1 = (nzh - 1 + 2 * u0) % nzh, (nzh - 1 + 2 * u1) % nzh
        second(0, own=True)
        relay(u0)
        first(d0, relayed=True)
        first(d1)
        third(0, own=True)
        weigh_all((0,), 0, nzh, True)
        second(d0)
        first(2, far=True)
        second(d1)
        third(d0)
        before = nzh * (1 - zh // 2)
        weigh_all((d0,), 0, before)
        second_panels(2)
        weigh_all((d0,), before, nzh)
        third(d1)
        third(2, far=True)
        late = (d1, 2)
    else:
        for d in near[1:]:
            first(d)
        for d in near:
            second(d, own=d == 0)
        third(0, own=True)
        weigh_all((0,), 0, nzh, True)
        for d in near[1:]:
            third(d)
        late = tuple(near[1:])

    def halves(e):
        zk = zof(e)

        for i in range(ny):
            d = direct[zk, i].reshape(rows, nnu).astype(BF16)
            val = vb[zk, i].reshape(nv, nnu)
            h = lax.dot_general(val, d, NT, preferred_element_type=F32)
            hs[zk, i] = h.astype(BF16).reshape(nzl, 2, 16, rows)
        send(hs.at[zk, :, :, 1 - co], c1.at[zk], h1s.at[0], h1r.at[e], partner)

    def over_zl(e):
        zk = zof(e)
        got(c1.at[zk], h1r.at[e])

        def add_core(i, carry):
            tsum[zk, :, i] = (hs[zk, i, :, co].astype(F32) + c1[zk, i].astype(F32)).astype(BF16)
            return carry

        lax.fori_loop(0, ny, add_core, 0)

        def h2(d):
            send(
                tsum.at[zk, (zl + d) % nzl], zr.at[zk, d], h2s.at[0], h2r.at[e], at_zl(d)
            )

        each(1, nzl, h2)

    def over_ka(e):
        zk = zof(e)
        if nzl > 1:
            got(zr.at[zk, 0 : nzl - 1], h2r.at[e])

        def add_zl(i, carry):
            total = tsum[zk, zl, i].astype(F32)
            for d in range(1, nzl):
                total = total + zr[zk, d, i].astype(F32)
            us[zk, i] = total.astype(BF16)
            return carry

        lax.fori_loop(0, ny, add_zl, 0)

        def h3(dy):
            send(
                us.at[zk, (y + dy) % ny], fr.at[zh, y], h3s.at[0 if e else 1], h3r.at[(nzh - e) % nzh],
                at_ka(dy, e),
            )

        each(1 if e == 0 else 0, ny, h3)
        if e == 0:
            fr[zh, y] = us[zh, y]

    far = near[::-1]
    for i, e in enumerate(far):
        if late:
            weigh(e, late)
        halves(e)
        if i:
            over_zl(far[i - 1])
    over_zl(far[-1])
    for e in far:
        over_ka(e)

    lane_b = lax.broadcasted_iota(jnp.int32, (16, rows), 1) // 32
    total = jnp.zeros((nzl * 16, nc), F32)
    for d in near[1:] + near[:1]:
        have = ny if d else ny - 1
        zs = zof(d)
        if have:
            got(fr.at[zs, 0:have], h3r.at[d])
        for i in range(ny):
            f = fr[zs, i].astype(F32)
            lhs = jnp.concatenate(
                [jnp.where(lane_b == b, f, 0.0) for b in range(nzl)], axis=0
            ).astype(BF16)
            total = total + jnp.dot(
                lhs, ct4[zs, i].reshape(rows, nc), preferred_element_type=F32
            )
    xs[r] = total.astype(BF16)

    def h5(d):
        send(xs.at[r], xs.at[r], h5s.at[0], h5r.at[0], at_row(d))

    each(1, nx, h5)

    legs = nzh - 1 if opposite else nzh
    if nzh > 1:
        got(vb.at[0 : len(beside) - 1, y, r], v1s.at[0])
        got(pb.at[0 : nzh - 1, :, zl, co], p1s.at[0])
        got(pb.at[0 : nzh - 1, :, :, co], pcs.at[0])
        got(fr.at[0 : nzh - 1], h3s.at[0])
        if nzl > 1:
            got(pb.at[0 : nzh - 1, :, 0 : nzl - 1, co], p2s.at[0])
    if ny > 1:
        got(pb.at[zh, 0 : ny - 1], p1s.at[1])
        got(fr.at[zh, 0 : ny - 1], h3s.at[1])
        got(vb.at[0:legs, 0 : ny - 1, r, 0], vas.at[0])
        got(vb.at[0:legs, 0 : ny - 1, :, 1], vds.at[0])
    if nx > 1:
        got(vb.at[0:legs, y, 0 : nx - 1, 1], vbs.at[0])
        got(vb.at[0:legs, :, 0 : nx - 1, 0], vcs.at[0])
    got(c1, h1s.at[0])
    if nzl > 1:
        got(zr.at[:, 0 : nzl - 1], h2s.at[0])
    if opposite:
        if ny > 1:
            got(vb.at[zh, 0 : ny - 1, r], vys.at[0])
        if nx > 1:
            got(vb.at[0 : nx - 1, :, r], vys.at[1])
        got(vb.at[zh, y, r, 0], vfs.at[0])
        got(prel.at[0], pfs.at[0])

        @pl.when(zh >= 2)
        def _():
            got(vb.at[zh, y, r], vgs.at[0])

    if nx > 1:
        got(xs.at[0 : nx - 1], h5r.at[0])
    result = xs[0].astype(F32)
    for i in range(1, nx):
        result = result + xs[i].astype(F32)
    out_ref[...] = (result * factor).reshape(out_ref.shape)

    if nx > 1:
        got(xs.at[0 : nx - 1], h5s.at[0])


def local(sizes, factor, exciton, orb_cond, orb_val, screened, q_table):
    ny, nzh, nx, nzl = sizes
    nka = ny * nzh
    legs = nzh - 1 if nzh > 2 else nzh
    nc = exciton.shape[-1]
    nv = nzl * 32
    rows = nzl * 32
    mu = nka * 32
    nnu = orb_val.shape[-1]
    any_space = pl.BlockSpec(memory_space=pl.ANY)
    dma = lambda *n: pltpu.SemaphoreType.DMA(n)
    vm = pltpu.VMEM
    out = pl.pallas_call(
        functools.partial(kernel, sizes, factor),
        name="isdf_direct",
        out_shape=jax.ShapeDtypeStruct((nzl, 16, nc), F32),
        in_specs=[any_space] * 5,
        out_specs=pl.BlockSpec(memory_space=pltpu.VMEM),
        scratch_shapes=[
            pltpu.SMEM((nka, nka), jnp.int32),
            vm((nzl, nv, nc), BF16),
            vm((nc, mu), BF16),
            vm((nka, 2, 16, nc), BF16),
            vm((nzh, ny, nzl, 32, nc), BF16),
            vm((nka, 32, nnu), BF16),
            vm((nka, 32, nnu), F32),
            vm((nka, 16, nv), BF16),
            vm((ny, nzl, 2, 16, nv), BF16),
            vm((2, max(1, ny // 2), 16, nv), BF16),
            vm((nzh, ny, nzl, 2, 16, nv), BF16),
            vm((nzh, ny, nx, 2, 16, nnu), BF16),
            vm((nzh, ny, nzl, 32, nnu), F32),
            vm((nzh, ny, nzl, 32, nnu), F32),
            vm((nzh, ny, nzl, 2, 16, rows), BF16),
            vm((nzh, ny, nzl, 16, rows), BF16),
            vm((nzh, nzl, ny, 16, rows), BF16),
            vm((nzh, nzl, ny, 16, rows), BF16),
            vm((nzh, ny, 16, rows), BF16),
            vm((nzh, ny, 16, rows), BF16),
            vm((nx, nzl * 16, nc), BF16),
            dma(5),
            dma(2), dma(nzh), dma(2), dma(1),
            dma(1), dma(max(1, nzh - 1)), dma(1), dma(max(1, nzh - 1)),
            dma(1), dma(max(1, nzh // 2)), dma(2), dma(1), dma(1), dma(2), dma(2),
            dma(1), dma(legs), dma(1), dma(legs),
            dma(1), dma(legs), dma(1), dma(legs),
            dma(1), dma(nzh), dma(1), dma(nzh),
            dma(2), dma(nzh), dma(1), dma(1),
        ],
        compiler_params=pltpu.CompilerParams(
            collective_id=0, has_side_effects=True, vmem_limit_bytes=56 * 1024 * 1024
        ),
    )(
        q_table,
        exciton[0],
        orb_cond[0],
        orb_val.reshape(nx, 2, 16, nnu),
        screened.reshape(nka, nka, 32, nnu),
    )
    return out[None]


def build(mesh, nzh, factor):
    shape = mesh.shape
    sizes = (shape["ka"] // nzh, nzh, shape["row"], shape["col"] // 2)
    placed = (
        P("ka", None, None, None),
        P("ka", None, "row"),
        P("ka", None, "col"),
        P(None, "row", "col"),
        P(),
    )
    return jax.shard_map(
        functools.partial(local, sizes, factor),
        mesh=mesh, in_specs=placed, out_specs=P("ka", None, "col", None), check_vma=False,
    )


def solution(mesh):
    return build(mesh, NZH, math.sqrt(128 * 128) / 2048)
```
